256 devices in a mesh: docs: 64 (over z, y, core), rep: 4 (over x).
Axes of the slice: x: 4, y: 4, z: 8, core: 2. Of those that a mesh axis runs over, the one named last changes fastest.
Arguments:
- queries: bfloat16 [32768, 1024], P(('docs', 'rep')), may hold values from -6 to 6
- adapter: bfloat16 [1024, 1024], replicated, may hold values from -0.1875 to 0.1875
- doc_table: bfloat16 [65536, 1024], P(('docs', 'rep')), may hold values from -6 to 6
- routes: int32 [32768, 4], P(('docs', 'rep')), may hold values from 0 to 255, all different within a row; in each aligned block of 128 rows (0 to 127, 128 to 255, ...) at most 4 rows name the same one
- doc_rows: int32 [32768, 4, 16], P(('docs', 'rep')), may hold values from 0 to 255, as said below
- labels: int32 [32768, 4, 16], P(('docs', 'rep')), may hold values from 0 to 4
Outputs:
- losses: float32 [32768], P(('docs', 'rep'))
- query_grads: bfloat16 [32768, 1024], P(('docs', 'rep'))
- adapter_grad: bfloat16 [1024, 1024], P('docs')
The draws below stay inside these ranges and needn't reach their ends.
Inputs may be any that keep to these rules, and one draw needn't show every extreme that they name: `routes`: each query names 4 different owners; among the queries of one device no owner is named more than 4 times, and in every draw some owner is named exactly 4 times by some device's queries. `doc_rows`: the 16 rows of one query at one owner are distinct.
All inputs are finite; a program needn't handle non-finite values.
Results may differ from the reference program's by a relative error of at most 0.024.
Values may be sent and summed in bfloat16 or wider, within the bound.
No kernel may reach another device: no remote copies, remote signals or barrier semaphores. Data moves between devices by JAX's collectives and lax.ppermute only.
A program may use at most 128 MiB of HBM per device.

```python
import math
import jax
import jax.numpy as jnp
import numpy as np
from jax import lax

D = 1024
QDEV = 128
DOC_DEV = 256
K = 4
M = 16
CAP = 4
QUERIES = 32768
NDOCS = 65536
DEVICES = 256


def draw_doc_rows(key, part):
    key_base, key_gaps = jax.random.split(key)
    start_rows = jax.random.randint(key_base, (QUERIES, K, 1), 0, DOC_DEV)
    gap_sizes = jax.random.randint(key_gaps, (QUERIES, K, M), 1, DOC_DEV // M + 1)
    offsets = jnp.cumsum(gap_sizes, axis=-1) - gap_sizes[:, :, :1]
    return ((start_rows + offsets) % DOC_DEV).astype(jnp.int32)


def place_ends(array, key, least, largest):
    extent = array.shape
    place = [jax.random.randint(jax.random.fold_in(key, axis), (), 0, extent[axis]) for axis in range(len(extent))]
    array = array.at[tuple(place)].set(least)
    longest = extent.index(max(extent))
    place[longest] = (place[longest] + 1) % extent[longest]
    return array.at[tuple(place)].set(largest)


def level_of(key, extent, shards, low, top_value):
    factor_of = 1.0
    for dim, shards_of in shards:
        steps = jax.random.uniform(jax.random.fold_in(jax.random.fold_in(key, 6), dim), (shards_of,), jnp.float32, low / len(shards), top_value / len(shards))
        factor_of = factor_of * jnp.repeat(jnp.exp(steps), extent[dim] // shards_of).reshape((-1,) + (1,) * (len(extent) - 1 - dim))
    return factor_of


def routed_block(own_key, own, number, rows, count, top, most, slope):
    sequence = jax.random.permutation(own_key, count)
    heavy_load, common = portions_of(count, rows * top, most, slope, True), portions_of(count, rows * top, most, slope, False)
    places = jnp.arange(count)

    def named(lengths, rotation):
        used = int((lengths > 0).sum())
        fixed = max(1, used // 4)
        shifted = fixed + (places - fixed + rotation * (used - fixed)) % max(1, count - fixed)
        return jnp.zeros((count,), jnp.int32).at[sequence[jnp.where(places < fixed, places, shifted)]].set(jnp.asarray(lengths, jnp.int32))

    lengths = jnp.where(number % 4 == 0, named(heavy_load, number // 4), named(common, number - number // 4 - 1))
    mixed = jax.random.permutation(jax.random.fold_in(own, 3), count)
    giver, sink = mixed[0:count // 2 * 2:2], mixed[1:count // 2 * 2:2]
    room = jnp.minimum(lengths[giver] - 1, most - lengths[sink]) // 2
    room = jnp.where((giver == sequence[0]) | (sink == sequence[0]) | (lengths[sink] == 0), 0, jnp.maximum(room, 0))
    shifted = jax.random.randint(jax.random.fold_in(own, 4), (count // 2,), 0, 1 << 20) % (room + 1)
    lengths = lengths.at[giver].add(-shifted).at[sink].add(shifted)
    members = jnp.searchsorted(jnp.cumsum(lengths), jnp.arange(rows * top), side="right").astype(jnp.int32)
    table = members.reshape(top, rows).T
    table = table[jax.random.permutation(jax.random.fold_in(own, 1), rows)]
    rotation = jax.random.randint(jax.random.fold_in(own, 2), (rows, 1), 0, top)
    return jnp.take_along_axis(table, (jnp.arange(top)[None, :] + rotation) % top, axis=1)


def portions_of(count, total, limit, slope, full):
    portions = [(1 << 20) // math.isqrt(rank ** slope) + 1 for rank in range(1, count + 1)]
    largest = limit if full else min(limit, max(-(-total // count), total * portions[0] // sum(portions)))
    least = 1 if total - largest >= count - 1 else 0
    counts, rest = [largest] + [least] * (count - 1), total - largest - least * (count - 1)
    while rest > 0:
        movable = [i for i in range(1, count) if counts[i] < largest] or [i for i in range(1, count) if counts[i] < limit]
        pool, budget = sum([portions[i] for i in movable]), rest
        for i in movable:
            more = min(limit - counts[i], max(1, budget * portions[i] // pool), rest)
            counts[i] = counts[i] + more
            rest = rest - more
    return np.array(counts)


def centred(rng, shape, scale, most, cuts=(), kind=jnp.bfloat16):
    result = scale * jax.random.normal(rng, shape, jnp.float32)
    if cuts:
        result = result * level_of(rng, shape, cuts, -0.22, 0.18)
    return jnp.clip(result, -most, most).astype(kind)


def setup_inputs(seed: int = 0) -> dict:
    streams_of = jax.random.split(jax.random.key(seed), 7)
    queries = centred(streams_of[0], (QUERIES, D), 1.0, 6.0, ((0, 256),))
    adapter = centred(streams_of[1], (D, D), D ** -0.5, 0.1875)
    doc_table = centred(streams_of[2], (NDOCS, D), 1.0, 6.0, ((0, 256),))
    routes_keys = jax.random.split(jax.random.fold_in(streams_of[3], 1), QUERIES // QDEV)
    routes_turns = jax.random.permutation(jax.random.fold_in(streams_of[3], 3), QUERIES // QDEV)
    routes = jax.vmap(lambda own, number: routed_block(jax.random.fold_in(streams_of[3], 2), own, number, QDEV, DEVICES, K, CAP, 1))(routes_keys, routes_turns).reshape((QUERIES, K))
    doc_rows = draw_doc_rows(jax.random.fold_in(streams_of[6], 71), 0)
    labels = place_ends(jax.random.randint(streams_of[5], (QUERIES, K, M), 0, 5), jax.random.fold_in(streams_of[5], 1), 0, 4).astype(jnp.int32)
    return dict(queries=queries, adapter=adapter, doc_table=doc_table, routes=routes, doc_rows=doc_rows, labels=labels)


EPSILON = 1e-06
LOSS_SCALE = 128.0

def unit_rows(rows):
    widened = rows.astype(jnp.float32)
    return (widened / jnp.sqrt(lax.optimization_barrier(jnp.mean(widened * widened, axis=-1, keepdims=True)) + EPSILON)).astype(jnp.bfloat16)

def reference(queries, adapter, doc_table, routes, doc_rows, labels):
    score_scale = 2.0 / math.sqrt(D)
    adapted = jnp.dot(queries, adapter, preferred_element_type=jnp.float32)
    radius = jnp.sqrt(lax.optimization_barrier(jnp.mean(adapted * adapted, axis=-1, keepdims=True)) + EPSILON)
    unit_exact = adapted / radius
    unit_query = unit_exact.astype(jnp.bfloat16)
    blocks = QUERIES // QDEV

    def one_block(pieces):
        unit_part, route_part, row_part, label_part = pieces
        cand_rows = route_part[:, :, None] * DOC_DEV + row_part
        candidates = unit_rows(doc_table[cand_rows]).astype(jnp.float32)
        scores = jnp.einsum('qd,qkmd->qkm', unit_part.astype(jnp.float32), candidates) * score_scale
        raised = jnp.exp(scores)
        norm_total = lax.optimization_barrier(jnp.sum(raised, axis=(1, 2)))
        label_weight = jnp.exp(label_part.astype(jnp.float32))
        target = label_weight / lax.optimization_barrier(jnp.sum(label_weight, axis=(1, 2), keepdims=True))
        losses = jnp.log(norm_total) - lax.optimization_barrier(jnp.sum(target * scores, axis=(1, 2)))
        weights = (LOSS_SCALE * (raised / norm_total[:, None, None] - target)).astype(jnp.bfloat16)
        pull_rows = (jnp.einsum('qkm,qkmd->qkd', weights.astype(jnp.float32), candidates) * score_scale).astype(jnp.bfloat16)
        pull_total = lax.optimization_barrier(jnp.sum(pull_rows.astype(jnp.float32), axis=1))
        return (losses, pull_total)
    losses, pull_total = lax.map(one_block, (unit_query.reshape(blocks, QDEV, D), routes.reshape(blocks, QDEV, K), doc_rows.reshape(blocks, QDEV, K, M), labels.reshape(blocks, QDEV, K, M)))
    losses = losses.reshape(QUERIES)
    pull_total = pull_total.reshape(QUERIES, D)
    projection = lax.optimization_barrier(jnp.mean(unit_exact * pull_total, axis=-1, keepdims=True))
    adapted_grad = ((pull_total - unit_exact * projection) / radius).astype(jnp.bfloat16)
    query_grads = lax.dot_general(adapted_grad, adapter, (((1,), (1,)), ((), ())), preferred_element_type=jnp.float32).astype(jnp.bfloat16)
    summed = lax.dot_general(queries, adapted_grad, (((0,), (0,)), ((), ())), preferred_element_type=jnp.float32)
    adapter_grad = (summed * (1.0 / math.sqrt(QUERIES))).astype(jnp.bfloat16)
    return (losses, query_grads, adapter_grad)
```

```python
import math

import jax
import jax.numpy as jnp
from jax import lax
from jax.experimental import pallas as pl
from jax.experimental.pallas import tpu as pltpu
from jax.sharding import Mesh
from jax.sharding import PartitionSpec as P

EPSILON = 1e-06
LOSS_SCALE = 128.0
F32 = jnp.float32
BF16 = jnp.bfloat16
TILE = 128
CORES = 2
CHIPS = ("z", "y", "rep")
DOCS = ("z", "y", "core")
EVERY = ("z", "y", "core", "rep")


def contract(left, right, left_dim, right_dim):
    return lax.dot_general(
        left, right, (((left_dim,), (right_dim,)), ((), ())), preferred_element_type=F32
    )


def ones_of(hit):
    return jnp.where(hit, 1.0, 0.0).astype(BF16)


def placed_of(target, slots):
    rows, fanout = target.shape
    index = lax.broadcasted_iota(jnp.int32, (rows, slots), 1)
    return [ones_of(index == target[:, k : k + 1]) for k in range(fanout)]


def by_owner(flat, fanout):
    rows = flat.shape[0]
    n = flat.shape[1] // fanout
    stacked = jnp.concatenate([flat[:, k * n : (k + 1) * n] for k in range(fanout)], axis=0)
    return jnp.concatenate([stacked, jnp.zeros((fanout * rows, TILE - n), stacked.dtype)], axis=1)


def unit_body(table, out):
    widened = table[...].astype(F32)
    out[...] = (
        widened / jnp.sqrt(jnp.mean(widened * widened, axis=-1, keepdims=True) + EPSILON)
    ).astype(BF16)


def send_body(queries, adapter, routes, doc_rows, out, exact_out, radius_out, target_out, *, owners, reps, capacity):
    rows, fanout = routes.shape
    width = queries.shape[1]
    adapted = contract(queries[...], adapter[...], 1, 0)
    radius = jnp.sqrt(jnp.mean(adapted * adapted, axis=-1, keepdims=True) + EPSILON)
    exact = adapted / radius
    exact_out[...] = exact
    radius_out[...] = radius
    owner_index = lax.broadcasted_iota(jnp.int32, (rows, owners), 1)
    hits = [jnp.where(owner_index == routes[:, k : k + 1], 1.0, 0.0) for k in range(fanout)]
    named = sum(hits).astype(BF16)
    lower = lax.broadcasted_iota(jnp.int32, (rows, rows), 0) > lax.broadcasted_iota(
        jnp.int32, (rows, rows), 1
    )
    earlier = contract(ones_of(lower), named, 1, 0)
    slot = jnp.concatenate(
        [jnp.sum(earlier * hit, axis=1, keepdims=True) for hit in hits], axis=1
    ).astype(jnp.int32)
    owner = routes[...]
    rep = owner % reps
    group = owner // reps
    core = group % CORES
    chip = (group // CORES) * reps + rep
    target = (chip * CORES + core) * capacity + slot
    target_out[...] = target
    placed = placed_of(target, owners * capacity)
    out[:, :width] = contract(sum(placed), exact.astype(BF16), 0, 0).astype(BF16)
    ids = by_owner(doc_rows[...].astype(F32).astype(BF16), fanout)
    out[:, width:] = contract(jnp.concatenate(placed, axis=0), ids, 0, 0).astype(BF16)


def score_body(place, arrived, own, other, scores_out, *, scale, capacity):
    width = own.shape[1]
    rows = arrived.shape[0]
    docs = own.shape[0]
    held = arrived[:, :width]
    core = (lax.broadcasted_iota(jnp.int32, (rows, docs), 0) // capacity) % CORES
    block = (
        jnp.where(core == place[0], contract(held, own[...], 1, 1), contract(held, other[...], 1, 1))
        * scale
    )
    wanted = arrived[:, width:].astype(F32).astype(jnp.int32)
    inner = wanted % TILE
    part = wanted // TILE
    picked = jnp.zeros((rows, TILE), F32)
    for t in range(docs // TILE):
        found = jnp.take_along_axis(block[:, t * TILE : (t + 1) * TILE], inner, axis=1)
        picked = jnp.where(part == t, found, picked)
    scores_out[...] = picked.astype(BF16)


def loss_body(returned, target, labels, losses_out, weights_out):
    fanout = target.shape[1]
    per_owner = labels.shape[1] // fanout
    placed = placed_of(target[...], returned.shape[0])
    scores = jnp.concatenate(
        [contract(one, returned[...], 1, 0)[:, :per_owner] for one in placed], axis=1
    )
    raised = jnp.exp(scores)
    norm_total = jnp.sum(raised, axis=1, keepdims=True)
    label_weight = jnp.exp(labels[...].astype(F32))
    label_share = label_weight / jnp.sum(label_weight, axis=1, keepdims=True)
    losses_out[...] = jnp.log(norm_total) - jnp.sum(label_share * scores, axis=1, keepdims=True)
    weights = (LOSS_SCALE * (raised / norm_total - label_share)).astype(BF16)
    weights_out[...] = contract(
        jnp.concatenate(placed, axis=0), by_owner(weights, fanout), 0, 0
    ).astype(BF16)


def pull_body(place, weights, arrived, own, other, out, *, scale, capacity, per_owner):
    docs, width = own.shape
    rows = arrived.shape[0]
    wanted = arrived[:, width:].astype(F32).T
    given = weights[...].astype(F32).T
    index = lax.broadcasted_iota(jnp.int32, (docs, rows), 0).astype(F32)
    spread = jnp.zeros((docs, rows), F32)
    for m in range(per_owner):
        spread = jnp.where(index == wanted[m : m + 1, :], given[m : m + 1, :], spread)
    core = (lax.broadcasted_iota(jnp.int32, (docs, rows), 1) // capacity) % CORES
    mine = core == place[0]
    near = jnp.where(mine, spread, 0.0).astype(BF16)
    far = jnp.where(mine, 0.0, spread).astype(BF16)
    out[...] = (
        (contract(near, own[...], 0, 0) + contract(far, other[...], 0, 0)) * scale
    ).astype(BF16)


def grad_body(place, pulled, target, exact, radius, queries, adapter, query_out, keep_out, give_out, terms):
    placed = sum(placed_of(target[...], pulled.shape[0]))
    pull_total = contract(placed, pulled[...], 1, 0)
    unit_exact = exact[...]
    projection = jnp.mean(unit_exact * pull_total, axis=-1, keepdims=True)
    adapted_grad = ((pull_total - unit_exact * projection) / radius[...]).astype(BF16)
    query_out[...] = contract(adapted_grad, adapter[...], 1, 1).astype(BF16)
    terms[...] = contract(queries[...], adapted_grad, 0, 0)
    ys, zs, block, _ = keep_out.shape
    core, y, z = place[0], place[1], place[2]
    for i in range(ys):
        for j in range(zs):
            group = (((z + j) % zs) * ys + (y + i) % ys) * CORES
            keep_out[i, j] = terms[pl.ds((group + core) * block, block), :].astype(BF16)
            give_out[i, j] = terms[pl.ds((group + 1 - core) * block, block), :].astype(BF16)


def call(body, name, outs, scratch=(), place=False):
    def run(*args):
        specs = [pl.BlockSpec(memory_space=pltpu.VMEM) for _ in args]
        if place:
            specs[0] = pl.BlockSpec(memory_space=pltpu.SMEM)
        return pl.pallas_call(
            body,
            name=name,
            in_specs=specs,
            out_shape=[jax.ShapeDtypeStruct(shape, dtype) for shape, dtype in outs],
            scratch_shapes=list(scratch),
        )(*args)

    return run


def exchange(rows, chips):
    grouped = rows.reshape(chips, rows.shape[0] // chips, rows.shape[1])
    return lax.all_to_all(grouped, CHIPS, split_axis=0, concat_axis=0, tiled=True).reshape(rows.shape)


def ahead(value, axis, step):
    size = lax.axis_size(axis)
    return lax.ppermute(value, axis, [(i, (i + step) % size) for i in range(size)])


def gather_steps(pieces, axis):
    got = [ahead(pieces[j], axis, j) for j in range(1, len(pieces))]
    total = pieces[0].astype(F32)
    for one in got:
        total = total + one.astype(F32)
    return total.astype(BF16)


def on_device(queries, adapter, doc_table, routes, doc_rows, labels):
    cores, reps = lax.axis_size("core"), lax.axis_size("rep")
    ys, zs = lax.axis_size("y"), lax.axis_size("z")
    owners = cores * reps * ys * zs
    chips = owners // cores
    query_rows, width = queries.shape
    fanout = routes.shape[1]
    per_owner = doc_rows.shape[2]
    docs = doc_table.shape[0]
    capacity = max(2, 2 * query_rows * fanout // owners)
    slots = owners * capacity
    scale = 2.0 / math.sqrt(width)
    flat_rows = doc_rows.reshape(query_rows, fanout * per_owner)
    flat_labels = labels.reshape(query_rows, fanout * per_owner)
    place = jnp.stack([lax.axis_index(name) for name in ("core", "y", "z")]).astype(jnp.int32)

    (own,) = call(unit_body, "unit", [((docs, width), BF16)])(doc_table)
    other = ahead(own, "core", 1)
    outgoing, exact, radius, target = call(
        lambda *refs: send_body(*refs, owners=owners, reps=reps, capacity=capacity),
        "send",
        [
            ((slots, width + TILE), BF16),
            ((query_rows, width), F32),
            ((query_rows, 1), F32),
            ((query_rows, fanout), jnp.int32),
        ],
    )(queries, adapter, routes, flat_rows)
    arrived = exchange(outgoing, chips)
    (scores_out,) = call(
        lambda *refs: score_body(*refs, scale=scale, capacity=capacity),
        "score",
        [((slots, TILE), BF16)],
        place=True,
    )(place, arrived, own, other)
    returned = exchange(scores_out, chips)
    losses, weights = call(loss_body, "loss", [((query_rows, 1), F32), ((slots, TILE), BF16)])(
        returned, target, flat_labels
    )
    weights_in = exchange(weights, chips)
    (pull_out,) = call(
        lambda *refs: pull_body(*refs, scale=scale, capacity=capacity, per_owner=per_owner),
        "pull",
        [((slots, width), BF16)],
        place=True,
    )(place, weights_in, arrived, own, other)
    pulled = exchange(pull_out, chips)
    block = width // (cores * ys * zs)
    query_grads, keep, give = call(
        grad_body,
        "grad",
        [((query_rows, width), BF16)] + [((ys, zs, block, width), BF16)] * 2,
        scratch=[pltpu.VMEM((width, width), F32)],
        place=True,
    )(place, pulled, target, exact, radius, queries, adapter)
    taken = ahead(give, "core", 1)
    pair = [(keep[i].astype(F32) + taken[i].astype(F32)).astype(BF16) for i in range(ys)]
    line = gather_steps(pair, "y")
    part = gather_steps([line[j] for j in range(zs)], "z")
    part = lax.optimization_barrier(part)
    got = [part] + [ahead(part, "rep", step) for step in range(1, reps)]
    half = max(1, reps // 2)
    sums = [sum(got[i + half * n].astype(F32) for n in range(reps // half)) for i in range(half)]
    adapter_grad = (sum(sums) * (1.0 / math.sqrt(query_rows * owners))).astype(BF16)
    return losses.reshape(query_rows), query_grads, adapter_grad


def solution(mesh):
    groups, reps = mesh.devices.shape
    ys = min(4, groups // CORES)
    fine = Mesh(mesh.devices.reshape(groups // (ys * CORES), ys, CORES, reps), EVERY)
    placed = (
        P(EVERY, None),
        P(),
        P(EVERY, None),
        P(EVERY, None),
        P(EVERY, None, None),
        P(EVERY, None, None),
    )
    return jax.shard_map(
        on_device,
        mesh=fine,
        in_specs=placed,
        out_specs=(P(EVERY), P(EVERY, None), P(DOCS, None)),
        check_vma=False,
    )
```

```python
import math

import jax
import jax.numpy as jnp
from jax import lax
from jax.experimental import pallas as pl
from jax.experimental.pallas import tpu as pltpu
from jax.sharding import Mesh
from jax.sharding import PartitionSpec as P

EPSILON = 1e-06
LOSS_SCALE = 128.0
F32 = jnp.float32
BF16 = jnp.bfloat16
TILE = 128
CORES = 2
CHIPS = ("z", "y", "rep")
DOCS = ("z", "y", "core")
EVERY = ("z", "y", "core", "rep")


def contract(left, right, left_dim, right_dim):
    return lax.dot_general(
        left, right, (((left_dim,), (right_dim,)), ((), ())), preferred_element_type=F32
    )


def ones_of(hit):
    return jnp.where(hit, 1.0, 0.0).astype(BF16)


def placed_of(target, slots):
    rows, fanout = target.shape
    index = lax.broadcasted_iota(jnp.int32, (rows, slots), 1)
    return [ones_of(index == target[:, k : k + 1]) for k in range(fanout)]


def by_owner(flat, fanout):
    n = flat.shape[1] // fanout
    return jnp.concatenate([flat[:, k * n : (k + 1) * n] for k in range(fanout)], axis=0)


def unit_body(table, out):
    widened = table[...].astype(F32)
    out[...] = (
        widened / jnp.sqrt(jnp.mean(widened * widened, axis=-1, keepdims=True) + EPSILON)
    ).astype(BF16)


def send_body(queries, adapter, routes, doc_rows, labels, out, exact_out, radius_out, target_out, *, owners, reps, capacity):
    rows, fanout = routes.shape
    width = queries.shape[1]
    adapted = contract(queries[...], adapter[...], 1, 0)
    radius = jnp.sqrt(jnp.mean(adapted * adapted, axis=-1, keepdims=True) + EPSILON)
    exact = adapted / radius
    exact_out[...] = exact
    radius_out[...] = radius
    owner_index = lax.broadcasted_iota(jnp.int32, (rows, owners), 1)
    hits = [jnp.where(owner_index == routes[:, k : k + 1], 1.0, 0.0) for k in range(fanout)]
    named = sum(hits).astype(BF16)
    lower = lax.broadcasted_iota(jnp.int32, (rows, rows), 0) > lax.broadcasted_iota(
        jnp.int32, (rows, rows), 1
    )
    earlier = contract(ones_of(lower), named, 1, 0)
    slot = jnp.concatenate(
        [jnp.sum(earlier * hit, axis=1, keepdims=True) for hit in hits], axis=1
    ).astype(jnp.int32)
    owner = routes[...]
    rep = owner % reps
    group = owner // reps
    core = group % CORES
    chip = (group // CORES) * reps + rep
    target = (chip * CORES + core) * capacity + slot
    target_out[...] = target
    placed = placed_of(target, owners * capacity)
    out[:, :width] = contract(sum(placed), exact.astype(BF16), 0, 0).astype(BF16)
    graded = labels[...].astype(F32)
    label_sum = jnp.sum(jnp.exp(graded), axis=1, keepdims=True)
    high = label_sum.astype(BF16).astype(F32)
    chunk = CORES * capacity
    shared = jnp.concatenate(
        [(target // chunk).astype(F32), (target % chunk).astype(F32), high, label_sum - high], axis=1
    )
    notes = jnp.concatenate(
        [
            by_owner(doc_rows[...].astype(F32), fanout),
            by_owner(graded, fanout),
            jnp.concatenate([shared] * fanout, axis=0),
        ],
        axis=1,
    )
    notes = jnp.concatenate(
        [notes, jnp.zeros((fanout * rows, TILE - notes.shape[1]), F32)], axis=1
    ).astype(BF16)
    out[:, width:] = contract(jnp.concatenate(placed, axis=0), notes, 0, 0).astype(BF16)


def score_body(place, arrived, own, other, stats_out, raised_out, share_out, notes_out, *, scale, capacity, fanout, per_owner):
    width = own.shape[1]
    rows = arrived.shape[0]
    docs = own.shape[0]
    held = arrived[:, :width]
    core = (lax.broadcasted_iota(jnp.int32, (rows, docs), 0) // capacity) % CORES
    block = (
        jnp.where(core == place[0], contract(held, own[...], 1, 1), contract(held, other[...], 1, 1))
        * scale
    )
    noted = arrived[:, width:].astype(F32)
    wanted = noted.astype(jnp.int32)
    inner = wanted % TILE
    part = wanted // TILE
    picked = jnp.zeros((rows, TILE), F32)
    for t in range(docs // TILE):
        found = jnp.take_along_axis(block[:, t * TILE : (t + 1) * TILE], inner, axis=1)
        picked = jnp.where(part == t, found, picked)
    notes = noted.T
    scores = picked.T[:per_owner, :]
    raised = jnp.exp(scores)
    label_weight = jnp.exp(notes[per_owner : 2 * per_owner, :])
    at = 2 * per_owner + 2 * fanout
    label_sum = notes[at : at + 1, :] + notes[at + 1 : at + 2, :]
    share = label_weight / jnp.where(label_sum > 0.0, label_sum, 1.0)
    raised_out[...] = raised
    share_out[...] = share
    notes_out[...] = notes[: notes_out.shape[0], :]
    norm_part = jnp.sum(raised, axis=0, keepdims=True)
    label_part = jnp.sum(share * scores, axis=0, keepdims=True)
    stats = jnp.concatenate(
        [v[:, i * TILE : (i + 1) * TILE] for v in (norm_part, label_part) for i in range(rows // TILE)],
        axis=0,
    )
    stats_out[...] = jnp.broadcast_to(stats[None], stats_out.shape).astype(BF16)


def loss_body(place, stats, target, losses_out, wide, *, chunk):
    rows, fanout = target.shape
    chips, lines, _ = stats.shape
    half = lines // 2
    wide[...] = stats[...].astype(F32).reshape(chips * lines, TILE)
    first = place[3] * chunk
    norm_rows = jnp.zeros((chips, TILE), F32)
    label_rows = jnp.zeros((chips, TILE), F32)
    for i in range(half):
        here = first // TILE == i
        norm_rows = jnp.where(here, wide[pl.ds(i, chips, stride=lines), :], norm_rows)
        label_rows = jnp.where(here, wide[pl.ds(half + i, chips, stride=lines), :], label_rows)
    lane = lax.broadcasted_iota(jnp.int32, (rows, TILE), 1)
    chip = lax.broadcasted_iota(jnp.int32, (rows, chips), 1)
    norm_total = jnp.zeros((rows, 1), F32)
    label_total = jnp.zeros((rows, 1), F32)
    for k in range(fanout):
        slot = target[:, k : k + 1]
        at = ones_of(chip == slot // chunk)
        mine = lane == first % TILE + slot % chunk
        for given, which in ((norm_rows, 0), (label_rows, 1)):
            found = jnp.where(mine, contract(at, given.astype(BF16), 1, 0), 0.0)
            found = jnp.sum(found, axis=1, keepdims=True)
            if which == 0:
                norm_total = norm_total + found
            else:
                label_total = label_total + found
    losses_out[...] = jnp.log(norm_total) - label_total


def pull_body(place, stats, notes, raised, share, own, other, out, wide, *, scale, capacity, fanout, per_owner):
    docs, width = own.shape
    rows = notes.shape[1]
    chunk = CORES * capacity
    chips, lines, _ = stats.shape
    wide[...] = stats[...].astype(F32).reshape(chips * lines, TILE)
    at = 2 * per_owner
    chip = lax.broadcasted_iota(jnp.int32, (chips, fanout * TILE), 0).astype(F32)
    line = lax.broadcasted_iota(jnp.int32, (TILE, fanout * TILE), 0)
    lane = lax.broadcasted_iota(jnp.int32, (1, TILE), 1)
    norms = []
    for i in range(rows // TILE):
        span = slice(i * TILE, (i + 1) * TILE)
        source = jnp.concatenate([notes[at + k : at + k + 1, span] for k in range(fanout)], axis=1)
        start = ((i * TILE + lane) // chunk) * chunk
        slot = jnp.concatenate(
            [
                (start + notes[at + fanout + k : at + fanout + k + 1, span].astype(jnp.int32)) % TILE
                for k in range(fanout)
            ],
            axis=1,
        )
        given = wide[pl.ds(i, chips, stride=lines), :].astype(BF16)
        found = jnp.where(line == slot, contract(given, ones_of(chip == source), 0, 0), 0.0)
        found = jnp.sum(found, axis=0, keepdims=True)
        norms.append(sum(found[:, k * TILE : (k + 1) * TILE] for k in range(fanout)))
    norm_total = jnp.concatenate(norms, axis=1)
    given = (LOSS_SCALE * (raised[...] / norm_total - share[...])).astype(BF16).astype(F32)
    index = lax.broadcasted_iota(jnp.int32, (docs, rows), 0).astype(F32)
    spread = jnp.zeros((docs, rows), F32)
    for m in range(per_owner):
        spread = jnp.where(index == notes[m : m + 1, :], given[m : m + 1, :], spread)
    core = (lax.broadcasted_iota(jnp.int32, (docs, rows), 1) // capacity) % CORES
    mine = core == place[0]
    near = jnp.where(mine, spread, 0.0).astype(BF16)
    far = jnp.where(mine, 0.0, spread).astype(BF16)
    out[...] = (
        (contract(near, own[...], 0, 0) + contract(far, other[...], 0, 0)) * scale
    ).astype(BF16)


def grad_body(place, pulled, target, exact, radius, queries, adapter, query_out, keep_out, give_out, terms):
    placed = sum(placed_of(target[...], pulled.shape[0]))
    pull_total = contract(placed, pulled[...], 1, 0)
    unit_exact = exact[...]
    projection = jnp.mean(unit_exact * pull_total, axis=-1, keepdims=True)
    adapted_grad = ((pull_total - unit_exact * projection) / radius[...]).astype(BF16)
    query_out[...] = contract(adapted_grad, adapter[...], 1, 1).astype(BF16)
    terms[...] = contract(queries[...], adapted_grad, 0, 0)
    ys, zs, block, _ = keep_out.shape
    core, y, z = place[0], place[1], place[2]
    for i in range(ys):
        for j in range(zs):
            group = (((z + j) % zs) * ys + (y + i) % ys) * CORES
            keep_out[i, j] = terms[pl.ds((group + core) * block, block), :].astype(BF16)
            give_out[i, j] = terms[pl.ds((group + 1 - core) * block, block), :].astype(BF16)


def call(body, name, outs, scratch=(), place=False):
    def run(*args):
        specs = [pl.BlockSpec(memory_space=pltpu.VMEM) for _ in args]
        if place:
            specs[0] = pl.BlockSpec(memory_space=pltpu.SMEM)
        return pl.pallas_call(
            body,
            name=name,
            in_specs=specs,
            out_shape=[jax.ShapeDtypeStruct(shape, dtype) for shape, dtype in outs],
            scratch_shapes=list(scratch),
        )(*args)

    return run


def exchange(rows, chips):
    grouped = rows.reshape(chips, rows.shape[0] // chips, rows.shape[1])
    return lax.all_to_all(grouped, CHIPS, split_axis=0, concat_axis=0, tiled=True).reshape(rows.shape)


def ahead(value, axis, step):
    size = lax.axis_size(axis)
    return lax.ppermute(value, axis, [(i, (i + step) % size) for i in range(size)])


def gather_steps(pieces, axis):
    got = [ahead(pieces[j], axis, j) for j in range(1, len(pieces))]
    total = pieces[0].astype(F32)
    for one in got:
        total = total + one.astype(F32)
    return total.astype(BF16)


def on_device(queries, adapter, doc_table, routes, doc_rows, labels):
    cores, reps = lax.axis_size("core"), lax.axis_size("rep")
    ys, zs = lax.axis_size("y"), lax.axis_size("z")
    owners = cores * reps * ys * zs
    chips = owners // cores
    query_rows, width = queries.shape
    fanout = routes.shape[1]
    per_owner = doc_rows.shape[2]
    docs = doc_table.shape[0]
    capacity = max(2, 2 * query_rows * fanout // owners)
    slots = owners * capacity
    scale = 2.0 / math.sqrt(width)
    flat_rows = doc_rows.reshape(query_rows, fanout * per_owner)
    flat_labels = labels.reshape(query_rows, fanout * per_owner)
    at = {name: lax.axis_index(name) for name in EVERY}
    chip = (at["z"] * ys + at["y"]) * reps + at["rep"]
    place = jnp.stack([at["core"], at["y"], at["z"], chip]).astype(jnp.int32)

    (own,) = call(unit_body, "unit", [((docs, width), BF16)])(doc_table)
    other = ahead(own, "core", 1)
    outgoing, exact, radius, target = call(
        lambda *refs: send_body(*refs, owners=owners, reps=reps, capacity=capacity),
        "send",
        [
            ((slots, width + TILE), BF16),
            ((query_rows, width), F32),
            ((query_rows, 1), F32),
            ((query_rows, fanout), jnp.int32),
        ],
    )(queries, adapter, routes, flat_rows, flat_labels)
    arrived = exchange(outgoing, chips)
    lines = 2 * slots // TILE
    noted = -(-(2 * per_owner + 2 * fanout) // 8) * 8
    stats_out, raised, share, notes = call(
        lambda *refs: score_body(
            *refs, scale=scale, capacity=capacity, fanout=fanout, per_owner=per_owner
        ),
        "score",
        [
            ((chips, lines, TILE), BF16),
            ((per_owner, slots), F32),
            ((per_owner, slots), F32),
            ((noted, slots), F32),
        ],
        place=True,
    )(place, arrived, own, other)
    stats = lax.all_to_all(stats_out, CHIPS, split_axis=0, concat_axis=0, tiled=True)
    wide = [pltpu.VMEM((chips * lines, TILE), F32)]
    (losses,) = call(
        lambda *refs: loss_body(*refs, chunk=CORES * capacity),
        "loss",
        [((query_rows, 1), F32)],
        scratch=wide,
        place=True,
    )(place, stats, target)
    (pull_out,) = call(
        lambda *refs: pull_body(
            *refs, scale=scale, capacity=capacity, fanout=fanout, per_owner=per_owner
        ),
        "pull",
        [((slots, width), BF16)],
        scratch=wide,
        place=True,
    )(place, stats, notes, raised, share, own, other)
    pulled = exchange(pull_out, chips)
    block = width // (cores * ys * zs)
    query_grads, keep, give = call(
        grad_body,
        "grad",
        [((query_rows, width), BF16)] + [((ys, zs, block, width), BF16)] * 2,
        scratch=[pltpu.VMEM((width, width), F32)],
        place=True,
    )(place, pulled, target, exact, radius, queries, adapter)
    taken = ahead(give, "core", 1)
    pair = [(keep[i].astype(F32) + taken[i].astype(F32)).astype(BF16) for i in range(ys)]
    line = gather_steps(pair, "y")
    part = gather_steps([line[j] for j in range(zs)], "z")
    part = lax.optimization_barrier(part)
    got = [part] + [ahead(part, "rep", step) for step in range(1, reps)]
    half = max(1, reps // 2)
    sums = [sum(got[i + half * n].astype(F32) for n in range(reps // half)) for i in range(half)]
    adapter_grad = (sum(sums) * (1.0 / math.sqrt(query_rows * owners))).astype(BF16)
    return losses.reshape(query_rows), query_grads, adapter_grad


def solution(mesh):
    groups, reps = mesh.devices.shape
    ys = min(4, groups // CORES)
    fine = Mesh(mesh.devices.reshape(groups // (ys * CORES), ys, CORES, reps), EVERY)
    placed = (
        P(EVERY, None),
        P(),
        P(EVERY, None),
        P(EVERY, None),
        P(EVERY, None, None),
        P(EVERY, None, None),
    )
    return jax.shard_map(
        on_device,
        mesh=fine,
        in_specs=placed,
        out_specs=(P(EVERY), P(EVERY, None), P(DOCS, None)),
        check_vma=False,
    )
```

```python
import math

import jax
import jax.numpy as jnp
from jax import lax
from jax.experimental import pallas as pl
from jax.experimental.pallas import tpu as pltpu
from jax.sharding import Mesh
from jax.sharding import PartitionSpec as P

EPSILON = 1e-06
LOSS_SCALE = 128.0
F32 = jnp.float32
BF16 = jnp.bfloat16
TILE = 128
CORES = 2
CHIPS = ("z", "y", "rep")
DOCS = ("z", "y", "core")
EVERY = ("z", "y", "core", "rep")


def contract(left, right, left_dim, right_dim):
    return lax.dot_general(
        left, right, (((left_dim,), (right_dim,)), ((), ())), preferred_element_type=F32
    )


def ones_of(hit):
    return jnp.where(hit, 1.0, 0.0).astype(BF16)


def placed_of(target, slots):
    rows, fanout = target.shape
    index = lax.broadcasted_iota(jnp.int32, (rows, slots), 1)
    return [ones_of(index == target[:, k : k + 1]) for k in range(fanout)]


def by_owner(flat, fanout):
    n = flat.shape[1] // fanout
    return jnp.concatenate([flat[:, k * n : (k + 1) * n] for k in range(fanout)], axis=0)


def unit_body(table, out):
    widened = table[...].astype(F32)
    out[...] = (
        widened / jnp.sqrt(jnp.mean(widened * widened, axis=-1, keepdims=True) + EPSILON)
    ).astype(BF16)


def adapt(rows, adapter):
    adapted = contract(rows, adapter, 1, 0)
    radius = jnp.sqrt(jnp.mean(adapted * adapted, axis=-1, keepdims=True) + EPSILON)
    return adapted / radius, radius


def local_body(queries, adapter, exact_out, radius_out):
    exact_out[...], radius_out[...] = adapt(queries[...], adapter[...])


def send_body(queries, routes, doc_rows, labels, out, target_out, *, owners, reps, capacity):
    rows, fanout = routes.shape
    width = queries.shape[1]
    owner_index = lax.broadcasted_iota(jnp.int32, (rows, owners), 1)
    hits = [jnp.where(owner_index == routes[:, k : k + 1], 1.0, 0.0) for k in range(fanout)]
    named = sum(hits).astype(BF16)
    lower = lax.broadcasted_iota(jnp.int32, (rows, rows), 0) > lax.broadcasted_iota(
        jnp.int32, (rows, rows), 1
    )
    earlier = contract(ones_of(lower), named, 1, 0)
    slot = jnp.concatenate(
        [jnp.sum(earlier * hit, axis=1, keepdims=True) for hit in hits], axis=1
    ).astype(jnp.int32)
    owner = routes[...]
    rep = owner % reps
    group = owner // reps
    core = group % CORES
    chip = (group // CORES) * reps + rep
    target = (chip * CORES + core) * capacity + slot
    target_out[...] = target
    placed = placed_of(target, owners * capacity)
    out[:, :width] = contract(sum(placed), queries[...], 0, 0).astype(BF16)
    graded = labels[...].astype(F32)
    label_sum = jnp.sum(jnp.exp(graded), axis=1, keepdims=True)
    high = label_sum.astype(BF16).astype(F32)
    chunk = CORES * capacity
    shared = jnp.concatenate(
        [(target // chunk).astype(F32), (target % chunk).astype(F32), high, label_sum - high], axis=1
    )
    notes = jnp.concatenate(
        [
            by_owner(doc_rows[...].astype(F32), fanout),
            by_owner(graded, fanout),
            jnp.concatenate([shared] * fanout, axis=0),
        ],
        axis=1,
    )
    notes = jnp.concatenate(
        [notes, jnp.zeros((fanout * rows, TILE - notes.shape[1]), F32)], axis=1
    ).astype(BF16)
    out[:, width:] = contract(jnp.concatenate(placed, axis=0), notes, 0, 0).astype(BF16)


def score_body(place, arrived, adapter, own, other, stats_out, raised_out, share_out, notes_out, *, scale, capacity, fanout, per_owner):
    width = own.shape[1]
    rows = arrived.shape[0]
    docs = own.shape[0]
    held = adapt(arrived[:, :width], adapter[...])[0].astype(BF16)
    core = (lax.broadcasted_iota(jnp.int32, (rows, docs), 0) // capacity) % CORES
    block = (
        jnp.where(core == place[0], contract(held, own[...], 1, 1), contract(held, other[...], 1, 1))
        * scale
    )
    noted = arrived[:, width:].astype(F32)
    wanted = noted.astype(jnp.int32)
    inner = wanted % TILE
    part = wanted // TILE
    picked = jnp.zeros((rows, TILE), F32)
    for t in range(docs // TILE):
        found = jnp.take_along_axis(block[:, t * TILE : (t + 1) * TILE], inner, axis=1)
        picked = jnp.where(part == t, found, picked)
    notes = noted.T
    scores = picked.T[:per_owner, :]
    raised = jnp.exp(scores)
    label_weight = jnp.exp(notes[per_owner : 2 * per_owner, :])
    at = 2 * per_owner + 2 * fanout
    label_sum = notes[at : at + 1, :] + notes[at + 1 : at + 2, :]
    share = label_weight / jnp.where(label_sum > 0.0, label_sum, 1.0)
    raised_out[...] = raised
    share_out[...] = share
    notes_out[...] = notes[: notes_out.shape[0], :]
    norm_part = jnp.sum(raised, axis=0, keepdims=True)
    label_part = jnp.sum(share * scores, axis=0, keepdims=True)
    stats = jnp.concatenate(
        [v[:, i * TILE : (i + 1) * TILE] for v in (norm_part, label_part) for i in range(rows // TILE)],
        axis=0,
    )
    stats_out[...] = jnp.broadcast_to(stats[None], stats_out.shape).astype(BF16)


def loss_body(place, stats, target, losses_out, wide, *, chunk):
    rows, fanout = target.shape
    chips, lines, _ = stats.shape
    half = lines // 2
    wide[...] = stats[...].astype(F32).reshape(chips * lines, TILE)
    first = place[3] * chunk
    norm_rows = jnp.zeros((chips, TILE), F32)
    label_rows = jnp.zeros((chips, TILE), F32)
    for i in range(half):
        here = first // TILE == i
        norm_rows = jnp.where(here, wide[pl.ds(i, chips, stride=lines), :], norm_rows)
        label_rows = jnp.where(here, wide[pl.ds(half + i, chips, stride=lines), :], label_rows)
    lane = lax.broadcasted_iota(jnp.int32, (rows, TILE), 1)
    chip = lax.broadcasted_iota(jnp.int32, (rows, chips), 1)
    norm_total = jnp.zeros((rows, 1), F32)
    label_total = jnp.zeros((rows, 1), F32)
    for k in range(fanout):
        slot = target[:, k : k + 1]
        at = ones_of(chip == slot // chunk)
        mine = lane == first % TILE + slot % chunk
        for given, which in ((norm_rows, 0), (label_rows, 1)):
            found = jnp.where(mine, contract(at, given.astype(BF16), 1, 0), 0.0)
            found = jnp.sum(found, axis=1, keepdims=True)
            if which == 0:
                norm_total = norm_total + found
            else:
                label_total = label_total + found
    losses_out[...] = jnp.log(norm_total) - label_total


def pull_body(place, stats, notes, raised, share, own, other, out, wide, *, scale, capacity, fanout, per_owner):
    docs, width = own.shape
    rows = notes.shape[1]
    chunk = CORES * capacity
    chips, lines, _ = stats.shape
    wide[...] = stats[...].astype(F32).reshape(chips * lines, TILE)
    at = 2 * per_owner
    chip = lax.broadcasted_iota(jnp.int32, (chips, fanout * TILE), 0).astype(F32)
    line = lax.broadcasted_iota(jnp.int32, (TILE, fanout * TILE), 0)
    lane = lax.broadcasted_iota(jnp.int32, (1, TILE), 1)
    norms = []
    for i in range(rows // TILE):
        span = slice(i * TILE, (i + 1) * TILE)
        source = jnp.concatenate([notes[at + k : at + k + 1, span] for k in range(fanout)], axis=1)
        start = ((i * TILE + lane) // chunk) * chunk
        slot = jnp.concatenate(
            [
                (start + notes[at + fanout + k : at + fanout + k + 1, span].astype(jnp.int32)) % TILE
                for k in range(fanout)
            ],
            axis=1,
        )
        given = wide[pl.ds(i, chips, stride=lines), :].astype(BF16)
        found = jnp.where(line == slot, contract(given, ones_of(chip == source), 0, 0), 0.0)
        found = jnp.sum(found, axis=0, keepdims=True)
        norms.append(sum(found[:, k * TILE : (k + 1) * TILE] for k in range(fanout)))
    norm_total = jnp.concatenate(norms, axis=1)
    given = (LOSS_SCALE * (raised[...] / norm_total - share[...])).astype(BF16).astype(F32)
    high = at + 2 * fanout
    given = jnp.where(notes[high : high + 1, :] > 0.0, given, 0.0)
    index = lax.broadcasted_iota(jnp.int32, (docs, rows), 0).astype(F32)
    spread = jnp.zeros((docs, rows), F32)
    for m in range(per_owner):
        spread = jnp.where(index == notes[m : m + 1, :], given[m : m + 1, :], spread)
    core = (lax.broadcasted_iota(jnp.int32, (docs, rows), 1) // capacity) % CORES
    mine = core == place[0]
    near = jnp.where(mine, spread, 0.0).astype(BF16)
    far = jnp.where(mine, 0.0, spread).astype(BF16)
    out[...] = (
        (contract(near, own[...], 0, 0) + contract(far, other[...], 0, 0)) * scale
    ).astype(BF16)


def terms_body(place, arrived, pulled, adapter, keep_out, give_out, terms):
    width = adapter.shape[0]
    held = arrived[:, :width]
    exact, radius = adapt(held, adapter[...])
    pull = pulled[...].astype(F32)
    projection = jnp.mean(exact * pull, axis=-1, keepdims=True)
    terms[...] = contract(held, ((pull - exact * projection) / radius).astype(BF16), 0, 0)
    ys, zs, block, _ = keep_out.shape
    core, y, z = place[0], place[1], place[2]
    for i in range(ys):
        for j in range(zs):
            group = (((z + j) % zs) * ys + (y + i) % ys) * CORES
            keep_out[i, j] = terms[pl.ds((group + core) * block, block), :].astype(BF16)
            give_out[i, j] = terms[pl.ds((group + 1 - core) * block, block), :].astype(BF16)


def grad_body(pulled, target, exact, radius, adapter, query_out):
    placed = sum(placed_of(target[...], pulled.shape[0]))
    pull_total = contract(placed, pulled[...], 1, 0)
    unit_exact = exact[...]
    projection = jnp.mean(unit_exact * pull_total, axis=-1, keepdims=True)
    adapted_grad = ((pull_total - unit_exact * projection) / radius[...]).astype(BF16)
    query_out[...] = contract(adapted_grad, adapter[...], 1, 1).astype(BF16)


def call(body, name, outs, scratch=(), place=False):
    def run(*args):
        specs = [pl.BlockSpec(memory_space=pltpu.VMEM) for _ in args]
        if place:
            specs[0] = pl.BlockSpec(memory_space=pltpu.SMEM)
        return pl.pallas_call(
            body,
            name=name,
            in_specs=specs,
            out_shape=[jax.ShapeDtypeStruct(shape, dtype) for shape, dtype in outs],
            scratch_shapes=list(scratch),
        )(*args)

    return run


def exchange(rows, chips):
    grouped = rows.reshape(chips, rows.shape[0] // chips, rows.shape[1])
    return lax.all_to_all(grouped, CHIPS, split_axis=0, concat_axis=0, tiled=True).reshape(rows.shape)


def ahead(value, axis, step):
    size = lax.axis_size(axis)
    return lax.ppermute(value, axis, [(i, (i + step) % size) for i in range(size)])


def gather_steps(pieces, axis):
    got = [ahead(pieces[j], axis, j) for j in range(1, len(pieces))]
    total = pieces[0].astype(F32)
    for one in got:
        total = total + one.astype(F32)
    return total.astype(BF16)


def on_device(queries, adapter, doc_table, routes, doc_rows, labels):
    cores, reps = lax.axis_size("core"), lax.axis_size("rep")
    ys, zs = lax.axis_size("y"), lax.axis_size("z")
    owners = cores * reps * ys * zs
    chips = owners // cores
    query_rows, width = queries.shape
    fanout = routes.shape[1]
    per_owner = doc_rows.shape[2]
    docs = doc_table.shape[0]
    capacity = max(2, 2 * query_rows * fanout // owners)
    slots = owners * capacity
    scale = 2.0 / math.sqrt(width)
    flat_rows = doc_rows.reshape(query_rows, fanout * per_owner)
    flat_labels = labels.reshape(query_rows, fanout * per_owner)
    at = {name: lax.axis_index(name) for name in EVERY}
    chip = (at["z"] * ys + at["y"]) * reps + at["rep"]
    place = jnp.stack([at["core"], at["y"], at["z"], chip]).astype(jnp.int32)

    (own,) = call(unit_body, "unit", [((docs, width), BF16)])(doc_table)
    other = ahead(own, "core", 1)
    outgoing, target = call(
        lambda *refs: send_body(*refs, owners=owners, reps=reps, capacity=capacity),
        "send",
        [((slots, width + TILE), BF16), ((query_rows, fanout), jnp.int32)],
    )(queries, routes, flat_rows, flat_labels)
    exact, radius = call(local_body, "local", [((query_rows, width), F32), ((query_rows, 1), F32)])(
        queries, adapter
    )
    arrived = exchange(outgoing, chips)
    lines = 2 * slots // TILE
    noted = -(-(2 * per_owner + 2 * fanout + 2) // 8) * 8
    stats_out, raised, share, notes = call(
        lambda *refs: score_body(
            *refs, scale=scale, capacity=capacity, fanout=fanout, per_owner=per_owner
        ),
        "score",
        [
            ((chips, lines, TILE), BF16),
            ((per_owner, slots), F32),
            ((per_owner, slots), F32),
            ((noted, slots), F32),
        ],
        place=True,
    )(place, arrived, adapter, own, other)
    stats = lax.all_to_all(stats_out, CHIPS, split_axis=0, concat_axis=0, tiled=True)
    wide = [pltpu.VMEM((chips * lines, TILE), F32)]
    (losses,) = call(
        lambda *refs: loss_body(*refs, chunk=CORES * capacity),
        "loss",
        [((query_rows, 1), F32)],
        scratch=wide,
        place=True,
    )(place, stats, target)
    (pull_out,) = call(
        lambda *refs: pull_body(
            *refs, scale=scale, capacity=capacity, fanout=fanout, per_owner=per_owner
        ),
        "pull",
        [((slots, width), BF16)],
        scratch=wide,
        place=True,
    )(place, stats, notes, raised, share, own, other)
    pulled = exchange(pull_out, chips)
    block = width // (cores * ys * zs)
    keep, give = call(
        terms_body,
        "terms",
        [((ys, zs, block, width), BF16)] * 2,
        scratch=[pltpu.VMEM((width, width), F32)],
        place=True,
    )(place, arrived, pull_out, adapter)
    (query_grads,) = call(grad_body, "grad", [((query_rows, width), BF16)])(
        pulled, target, exact, radius, adapter
    )
    taken = ahead(give, "core", 1)
    pair = [(keep[i].astype(F32) + taken[i].astype(F32)).astype(BF16) for i in range(ys)]
    line = gather_steps(pair, "y")
    part = gather_steps([line[j] for j in range(zs)], "z")
    part = lax.optimization_barrier(part)
    got = [part] + [ahead(part, "rep", step) for step in range(1, reps)]
    half = max(1, reps // 2)
    sums = [sum(got[i + half * n].astype(F32) for n in range(reps // half)) for i in range(half)]
    adapter_grad = (sum(sums) * (1.0 / math.sqrt(query_rows * owners))).astype(BF16)
    return losses.reshape(query_rows), query_grads, adapter_grad


def solution(mesh):
    groups, reps = mesh.devices.shape
    ys = min(4, groups // CORES)
    fine = Mesh(mesh.devices.reshape(groups // (ys * CORES), ys, CORES, reps), EVERY)
    placed = (
        P(EVERY, None),
        P(),
        P(EVERY, None),
        P(EVERY, None),
        P(EVERY, None, None),
        P(EVERY, None, None),
    )
    return jax.shard_map(
        on_device,
        mesh=fine,
        in_specs=placed,
        out_specs=(P(EVERY), P(EVERY, None), P(DOCS, None)),
        check_vma=False,
    )
```

```python
import math

import jax
import jax.numpy as jnp
from jax import lax
from jax.experimental import pallas as pl
from jax.experimental.pallas import tpu as pltpu
from jax.sharding import Mesh
from jax.sharding import PartitionSpec as P

EPSILON = 1e-06
LOSS_SCALE = 128.0
F32 = jnp.float32
BF16 = jnp.bfloat16
TILE = 128
CORES = 2
CHIPS = ("z", "y", "rep")
DOCS = ("z", "y", "core")
EVERY = ("z", "y", "core", "rep")


def contract(left, right, left_dim, right_dim):
    return lax.dot_general(
        left, right, (((left_dim,), (right_dim,)), ((), ())), preferred_element_type=F32
    )


def ones_of(hit):
    return jnp.where(hit, 1.0, 0.0).astype(BF16)


def placed_of(target, slots):
    rows, fanout = target.shape
    index = lax.broadcasted_iota(jnp.int32, (rows, slots), 1)
    return [ones_of(index == target[:, k : k + 1]) for k in range(fanout)]


def by_owner(flat, fanout):
    n = flat.shape[1] // fanout
    return jnp.concatenate([flat[:, k * n : (k + 1) * n] for k in range(fanout)], axis=0)


def unit_body(table, out):
    widened = table[...].astype(F32)
    out[...] = (
        widened / jnp.sqrt(jnp.mean(widened * widened, axis=-1, keepdims=True) + EPSILON)
    ).astype(BF16)


def adapt(rows, adapter):
    adapted = contract(rows, adapter, 1, 0)
    radius = jnp.sqrt(jnp.mean(adapted * adapted, axis=-1, keepdims=True) + EPSILON)
    return adapted / radius, radius


def local_body(queries, adapter, exact_out, radius_out):
    exact_out[...], radius_out[...] = adapt(queries[...], adapter[...])


def send_body(queries, routes, doc_rows, labels, out, target_out, *, owners, reps, capacity):
    fanout, rows = routes.shape
    width = queries.shape[1]
    blank = jnp.zeros((TILE - fanout, rows), F32)
    named_owners = jnp.concatenate([routes[...].astype(F32), blank], axis=0).T[:, :fanout]
    named_owners = named_owners.astype(jnp.int32)
    owner_index = lax.broadcasted_iota(jnp.int32, (rows, owners), 1)
    hits = [jnp.where(owner_index == named_owners[:, k : k + 1], 1.0, 0.0) for k in range(fanout)]
    named = sum(hits).astype(BF16)
    lower = lax.broadcasted_iota(jnp.int32, (rows, rows), 0) > lax.broadcasted_iota(
        jnp.int32, (rows, rows), 1
    )
    earlier = contract(ones_of(lower), named, 1, 0)
    slot = jnp.concatenate(
        [jnp.sum(earlier * hit, axis=1, keepdims=True) for hit in hits], axis=1
    ).astype(jnp.int32)
    owner = named_owners
    rep = owner % reps
    group = owner // reps
    core = group % CORES
    chip = (group // CORES) * reps + rep
    target = (chip * CORES + core) * capacity + slot
    target_out[...] = target
    placed = placed_of(target, owners * capacity)
    out[:, :width] = contract(sum(placed), queries[...], 0, 0).astype(BF16)
    graded = labels[...].astype(F32).T
    label_sum = jnp.sum(jnp.exp(graded), axis=1, keepdims=True)
    high = label_sum.astype(BF16).astype(F32)
    chunk = CORES * capacity
    shared = jnp.concatenate(
        [(target // chunk).astype(F32), (target % chunk).astype(F32), high, label_sum - high], axis=1
    )
    notes = jnp.concatenate(
        [
            by_owner(doc_rows[...].astype(F32).T, fanout),
            by_owner(graded, fanout),
            jnp.concatenate([shared] * fanout, axis=0),
        ],
        axis=1,
    )
    notes = jnp.concatenate(
        [notes, jnp.zeros((fanout * rows, TILE - notes.shape[1]), F32)], axis=1
    ).astype(BF16)
    out[:, width:] = contract(jnp.concatenate(placed, axis=0), notes, 0, 0).astype(BF16)


def score_body(place, arrived, adapter, own, other, stats_out, raised_out, share_out, notes_out, *, scale, capacity, fanout, per_owner):
    width = own.shape[1]
    rows = arrived.shape[0]
    docs = own.shape[0]
    held = adapt(arrived[:, :width], adapter[...])[0].astype(BF16)
    core = (lax.broadcasted_iota(jnp.int32, (rows, docs), 0) // capacity) % CORES
    block = (
        jnp.where(core == place[0], contract(held, own[...], 1, 1), contract(held, other[...], 1, 1))
        * scale
    )
    noted = arrived[:, width:].astype(F32)
    wanted = noted.astype(jnp.int32)
    inner = wanted % TILE
    part = wanted // TILE
    picked = jnp.zeros((rows, TILE), F32)
    for t in range(docs // TILE):
        found = jnp.take_along_axis(block[:, t * TILE : (t + 1) * TILE], inner, axis=1)
        picked = jnp.where(part == t, found, picked)
    notes = noted.T
    scores = picked.T[:per_owner, :]
    raised = jnp.exp(scores)
    label_weight = jnp.exp(notes[per_owner : 2 * per_owner, :])
    at = 2 * per_owner + 2 * fanout
    label_sum = notes[at : at + 1, :] + notes[at + 1 : at + 2, :]
    share = label_weight / jnp.where(label_sum > 0.0, label_sum, 1.0)
    raised_out[...] = raised
    share_out[...] = share
    notes_out[...] = notes[: notes_out.shape[0], :]
    norm_part = jnp.sum(raised, axis=0, keepdims=True)
    label_part = jnp.sum(share * scores, axis=0, keepdims=True)
    stats = jnp.concatenate(
        [v[:, i * TILE : (i + 1) * TILE] for v in (norm_part, label_part) for i in range(rows // TILE)],
        axis=0,
    )
    stats_out[...] = jnp.broadcast_to(stats[None], stats_out.shape).astype(BF16)


def loss_body(place, stats, target, losses_out, wide, *, chunk):
    rows, fanout = target.shape
    chips, lines, _ = stats.shape
    half = lines // 2
    wide[...] = stats[...].astype(F32).reshape(chips * lines, TILE)
    first = place[3] * chunk
    norm_rows = jnp.zeros((chips, TILE), F32)
    label_rows = jnp.zeros((chips, TILE), F32)
    for i in range(half):
        here = first // TILE == i
        norm_rows = jnp.where(here, wide[pl.ds(i, chips, stride=lines), :], norm_rows)
        label_rows = jnp.where(here, wide[pl.ds(half + i, chips, stride=lines), :], label_rows)
    lane = lax.broadcasted_iota(jnp.int32, (rows, TILE), 1)
    chip = lax.broadcasted_iota(jnp.int32, (rows, chips), 1)
    norm_total = jnp.zeros((rows, 1), F32)
    label_total = jnp.zeros((rows, 1), F32)
    for k in range(fanout):
        slot = target[:, k : k + 1]
        at = ones_of(chip == slot // chunk)
        mine = lane == first % TILE + slot % chunk
        for given, which in ((norm_rows, 0), (label_rows, 1)):
            found = jnp.where(mine, contract(at, given.astype(BF16), 1, 0), 0.0)
            found = jnp.sum(found, axis=1, keepdims=True)
            if which == 0:
                norm_total = norm_total + found
            else:
                label_total = label_total + found
    losses = jnp.broadcast_to(jnp.log(norm_total) - label_total, (rows, TILE))
    losses_out[...] = losses.T[0:1, :]


def pull_body(place, stats, notes, raised, share, own, other, out, wide, *, scale, capacity, fanout, per_owner):
    docs, width = own.shape
    rows = notes.shape[1]
    chunk = CORES * capacity
    chips, lines, _ = stats.shape
    wide[...] = stats[...].astype(F32).reshape(chips * lines, TILE)
    at = 2 * per_owner
    chip = lax.broadcasted_iota(jnp.int32, (chips, fanout * TILE), 0).astype(F32)
    line = lax.broadcasted_iota(jnp.int32, (TILE, fanout * TILE), 0)
    lane = lax.broadcasted_iota(jnp.int32, (1, TILE), 1)
    norms = []
    for i in range(rows // TILE):
        span = slice(i * TILE, (i + 1) * TILE)
        source = jnp.concatenate([notes[at + k : at + k + 1, span] for k in range(fanout)], axis=1)
        start = ((i * TILE + lane) // chunk) * chunk
        slot = jnp.concatenate(
            [
                (start + notes[at + fanout + k : at + fanout + k + 1, span].astype(jnp.int32)) % TILE
                for k in range(fanout)
            ],
            axis=1,
        )
        given = wide[pl.ds(i, chips, stride=lines), :].astype(BF16)
        found = jnp.where(line == slot, contract(given, ones_of(chip == source), 0, 0), 0.0)
        found = jnp.sum(found, axis=0, keepdims=True)
        norms.append(sum(found[:, k * TILE : (k + 1) * TILE] for k in range(fanout)))
    norm_total = jnp.concatenate(norms, axis=1)
    given = (LOSS_SCALE * (raised[...] / norm_total - share[...])).astype(BF16).astype(F32)
    high = at + 2 * fanout
    given = jnp.where(notes[high : high + 1, :] > 0.0, given, 0.0)
    index = lax.broadcasted_iota(jnp.int32, (docs, rows), 0).astype(F32)
    spread = jnp.zeros((docs, rows), F32)
    for m in range(per_owner):
        spread = jnp.where(index == notes[m : m + 1, :], given[m : m + 1, :], spread)
    core = (lax.broadcasted_iota(jnp.int32, (docs, rows), 1) // capacity) % CORES
    mine = core == place[0]
    near = jnp.where(mine, spread, 0.0).astype(BF16)
    far = jnp.where(mine, 0.0, spread).astype(BF16)
    out[...] = (
        (contract(near, own[...], 0, 0) + contract(far, other[...], 0, 0)) * scale
    ).astype(BF16)


def ready_body(arrived, adapter, exact_out, radius_out):
    exact_out[...], radius_out[...] = adapt(arrived[:, : adapter.shape[0]], adapter[...])


def terms_body(place, arrived, exact, radius, pulled, keep_out, give_out, terms):
    width = pulled.shape[1]
    pull = pulled[...].astype(F32)
    projection = jnp.mean(exact[...] * pull, axis=-1, keepdims=True)
    owed = ((pull - exact[...] * projection) / radius[...]).astype(BF16)
    terms[...] = contract(arrived[:, :width], owed, 0, 0)
    ys, zs, block, _ = keep_out.shape
    core, y, z = place[0], place[1], place[2]
    for i in range(ys):
        for j, far in enumerate(halving(zs)):
            group = ((z ^ far) * ys + (y + i) % ys) * CORES
            keep_out[i, j] = terms[pl.ds((group + core) * block, block), :].astype(BF16)
            give_out[i, j] = terms[pl.ds((group + 1 - core) * block, block), :].astype(BF16)


def grad_body(pulled, target, exact, radius, adapter, query_out):
    placed = sum(placed_of(target[...], pulled.shape[0]))
    pull_total = contract(placed, pulled[...], 1, 0)
    unit_exact = exact[...]
    projection = jnp.mean(unit_exact * pull_total, axis=-1, keepdims=True)
    adapted_grad = ((pull_total - unit_exact * projection) / radius[...]).astype(BF16)
    query_out[...] = contract(adapted_grad, adapter[...], 1, 1).astype(BF16)


def halving(size):
    order = [0]
    bit = size // 2
    while bit:
        order = order + [one + bit for one in order]
        bit //= 2
    return order


def call(body, name, outs, scratch=(), place=False):
    def run(*args):
        specs = [pl.BlockSpec(memory_space=pltpu.VMEM) for _ in args]
        if place:
            specs[0] = pl.BlockSpec(memory_space=pltpu.SMEM)
        return pl.pallas_call(
            body,
            name=name,
            in_specs=specs,
            out_shape=[jax.ShapeDtypeStruct(shape, dtype) for shape, dtype in outs],
            scratch_shapes=list(scratch),
        )(*args)

    return run


def exchange(rows, chips):
    grouped = rows.reshape(chips, rows.shape[0] // chips, rows.shape[1])
    return lax.all_to_all(grouped, CHIPS, split_axis=0, concat_axis=0, tiled=True).reshape(rows.shape)


def ahead(value, axis, step):
    size = lax.axis_size(axis)
    return lax.ppermute(value, axis, [(i, (i + step) % size) for i in range(size)])


def added(pieces):
    total = pieces[0].astype(F32)
    for one in pieces[1:]:
        total = total + one.astype(F32)
    return total.astype(BF16)


def halved(value, axis):
    bit = 1
    size = lax.axis_size(axis)
    while value.shape[0] > 1:
        half = value.shape[0] // 2
        got = lax.ppermute(value[half:], axis, [(i, i ^ bit) for i in range(size)])
        value = added([value[:half], got])
        bit *= 2
    return value[0]


def on_device(queries, adapter, doc_table, routes, doc_rows, labels):
    cores, reps = lax.axis_size("core"), lax.axis_size("rep")
    ys, zs = lax.axis_size("y"), lax.axis_size("z")
    owners = cores * reps * ys * zs
    chips = owners // cores
    query_rows, width = queries.shape
    fanout = routes.shape[1]
    per_owner = doc_rows.shape[2]
    docs = doc_table.shape[0]
    capacity = max(2, 2 * query_rows * fanout // owners)
    slots = owners * capacity
    scale = 2.0 / math.sqrt(width)
    flat_rows = doc_rows.transpose(1, 2, 0).reshape(fanout * per_owner, query_rows)
    flat_labels = labels.transpose(1, 2, 0).reshape(fanout * per_owner, query_rows)
    at = {name: lax.axis_index(name) for name in EVERY}
    chip = (at["z"] * ys + at["y"]) * reps + at["rep"]
    place = jnp.stack([at["core"], at["y"], at["z"], chip]).astype(jnp.int32)

    (own,) = call(unit_body, "unit", [((docs, width), BF16)])(doc_table)
    other = ahead(own, "core", 1)
    outgoing, target = call(
        lambda *refs: send_body(*refs, owners=owners, reps=reps, capacity=capacity),
        "send",
        [((slots, width + TILE), BF16), ((query_rows, fanout), jnp.int32)],
    )(queries, routes.T, flat_rows, flat_labels)
    exact, radius = call(local_body, "local", [((query_rows, width), F32), ((query_rows, 1), F32)])(
        queries, adapter
    )
    arrived = exchange(outgoing, chips)
    arrived, exact, radius = lax.optimization_barrier((arrived, exact, radius))
    lines = 2 * slots // TILE
    noted = -(-(2 * per_owner + 2 * fanout + 2) // 8) * 8
    stats_out, raised, share, notes = call(
        lambda *refs: score_body(
            *refs, scale=scale, capacity=capacity, fanout=fanout, per_owner=per_owner
        ),
        "score",
        [
            ((chips, lines, TILE), BF16),
            ((per_owner, slots), F32),
            ((per_owner, slots), F32),
            ((noted, slots), F32),
        ],
        place=True,
    )(place, arrived, adapter, own, other)
    stats = lax.all_to_all(stats_out, CHIPS, split_axis=0, concat_axis=0, tiled=True)
    held_exact, held_radius = call(ready_body, "ready", [((slots, width), F32), ((slots, 1), F32)])(
        arrived, adapter
    )
    stats, held_exact, held_radius = lax.optimization_barrier((stats, held_exact, held_radius))
    wide = [pltpu.VMEM((chips * lines, TILE), F32)]
    (losses,) = call(
        lambda *refs: loss_body(*refs, chunk=CORES * capacity),
        "loss",
        [((1, query_rows), F32)],
        scratch=wide,
        place=True,
    )(place, stats, target)
    (pull_out,) = call(
        lambda *refs: pull_body(
            *refs, scale=scale, capacity=capacity, fanout=fanout, per_owner=per_owner
        ),
        "pull",
        [((slots, width), BF16)],
        scratch=wide,
        place=True,
    )(place, stats, notes, raised, share, own, other)
    pulled = exchange(pull_out, chips)
    block = width // (cores * ys * zs)
    keep, give = call(
        terms_body,
        "terms",
        [((ys, zs, block, width), BF16)] * 2,
        scratch=[pltpu.VMEM((width, width), F32)],
        place=True,
    )(place, arrived, held_exact, held_radius, pull_out)
    (query_grads,) = call(grad_body, "grad", [((query_rows, width), BF16)])(
        pulled, target, exact, radius, adapter
    )
    taken = ahead(give, "core", 1)
    pair = [(keep[i].astype(F32) + taken[i].astype(F32)).astype(BF16) for i in range(ys)]
    line = [ahead(pair[j], "y", j) for j in range(1, ys)]
    line, losses = lax.optimization_barrier((line, losses))
    part = halved(added(pair[:1] + line), "z")
    part = lax.optimization_barrier(part)
    got = [part] + [ahead(part, "rep", step) for step in range(1, reps)]
    half = max(1, reps // 2)
    sums = [sum(got[i + half * n].astype(F32) for n in range(reps // half)) for i in range(half)]
    adapter_grad = (sum(sums) * (1.0 / math.sqrt(query_rows * owners))).astype(BF16)
    return losses.reshape(query_rows), query_grads, adapter_grad


def solution(mesh):
    groups, reps = mesh.devices.shape
    ys = min(4, groups // CORES)
    fine = Mesh(mesh.devices.reshape(groups // (ys * CORES), ys, CORES, reps), EVERY)
    placed = (
        P(EVERY, None),
        P(),
        P(EVERY, None),
        P(EVERY, None),
        P(EVERY, None, None),
        P(EVERY, None, None),
    )
    return jax.shard_map(
        on_device,
        mesh=fine,
        in_specs=placed,
        out_specs=(P(EVERY), P(EVERY, None), P(DOCS, None)),
        check_vma=False,
    )
```

```python
import math

import jax
import jax.numpy as jnp
from jax import lax
from jax.experimental import pallas as pl
from jax.experimental.pallas import tpu as pltpu
from jax.sharding import Mesh
from jax.sharding import PartitionSpec as P

EPSILON = 1e-06
LOSS_SCALE = 128.0
F32 = jnp.float32
BF16 = jnp.bfloat16
TILE = 128
CORES = 2
CHIPS = ("z", "y", "rep")
DOCS = ("z", "y", "core")
EVERY = ("z", "y", "core", "rep")


def contract(left, right, left_dim, right_dim):
    return lax.dot_general(
        left, right, (((left_dim,), (right_dim,)), ((), ())), preferred_element_type=F32
    )


def ones_of(hit):
    return jnp.where(hit, 1.0, 0.0).astype(BF16)


def placed_of(target, slots):
    rows, fanout = target.shape
    index = lax.broadcasted_iota(jnp.int32, (rows, slots), 1)
    return [ones_of(index == target[:, k : k + 1]) for k in range(fanout)]


def by_owner(flat, fanout):
    n = flat.shape[1] // fanout
    return jnp.concatenate([flat[:, k * n : (k + 1) * n] for k in range(fanout)], axis=0)


def unit_body(table, out):
    widened = table[...].astype(F32)
    out[...] = (
        widened / jnp.sqrt(jnp.mean(widened * widened, axis=-1, keepdims=True) + EPSILON)
    ).astype(BF16)


def adapt(rows, adapter):
    adapted = contract(rows, adapter, 1, 0)
    radius = jnp.sqrt(jnp.mean(adapted * adapted, axis=-1, keepdims=True) + EPSILON)
    return adapted / radius, radius


def local_body(queries, adapter, exact_out, radius_out):
    exact_out[...], radius_out[...] = adapt(queries[...], adapter[...])


def send_body(queries, routes, doc_rows, labels, out, target_out, *, owners, reps, capacity):
    fanout, rows = routes.shape
    width = queries.shape[1]
    blank = jnp.zeros((TILE - fanout, rows), F32)
    named_owners = jnp.concatenate([routes[...].astype(F32), blank], axis=0).T[:, :fanout]
    named_owners = named_owners.astype(jnp.int32)
    owner_index = lax.broadcasted_iota(jnp.int32, (rows, owners), 1)
    hits = [jnp.where(owner_index == named_owners[:, k : k + 1], 1.0, 0.0) for k in range(fanout)]
    named = sum(hits).astype(BF16)
    lower = lax.broadcasted_iota(jnp.int32, (rows, rows), 0) > lax.broadcasted_iota(
        jnp.int32, (rows, rows), 1
    )
    earlier = contract(ones_of(lower), named, 1, 0)
    slot = jnp.concatenate(
        [jnp.sum(earlier * hit, axis=1, keepdims=True) for hit in hits], axis=1
    ).astype(jnp.int32)
    owner = named_owners
    rep = owner % reps
    group = owner // reps
    core = group % CORES
    chip = (group // CORES) * reps + rep
    target = (chip * CORES + core) * capacity + slot
    target_out[...] = target
    placed = placed_of(target, owners * capacity)
    out[:, :width] = contract(sum(placed), queries[...], 0, 0).astype(BF16)
    graded = labels[...].astype(F32).T
    label_sum = jnp.sum(jnp.exp(graded), axis=1, keepdims=True)
    high = label_sum.astype(BF16).astype(F32)
    chunk = CORES * capacity
    shared = jnp.concatenate(
        [(target // chunk).astype(F32), (target % chunk).astype(F32), high, label_sum - high], axis=1
    )
    notes = jnp.concatenate(
        [
            by_owner(doc_rows[...].astype(F32).T, fanout),
            by_owner(graded, fanout),
            jnp.concatenate([shared] * fanout, axis=0),
        ],
        axis=1,
    )
    notes = jnp.concatenate(
        [notes, jnp.zeros((fanout * rows, TILE - notes.shape[1]), F32)], axis=1
    ).astype(BF16)
    out[:, width:] = contract(jnp.concatenate(placed, axis=0), notes, 0, 0).astype(BF16)


def score_body(place, arrived, adapter, own, other, stats_out, raised_out, share_out, notes_out, *, scale, capacity, fanout, per_owner):
    width = own.shape[1]
    rows = arrived.shape[0]
    docs = own.shape[0]
    held = adapt(arrived[:, :width], adapter[...])[0].astype(BF16)
    core = (lax.broadcasted_iota(jnp.int32, (rows, docs), 0) // capacity) % CORES
    block = (
        jnp.where(core == place[0], contract(held, own[...], 1, 1), contract(held, other[...], 1, 1))
        * scale
    )
    noted = arrived[:, width:].astype(F32)
    wanted = noted.astype(jnp.int32)
    inner = wanted % TILE
    part = wanted // TILE
    picked = jnp.zeros((rows, TILE), F32)
    for t in range(docs // TILE):
        found = jnp.take_along_axis(block[:, t * TILE : (t + 1) * TILE], inner, axis=1)
        picked = jnp.where(part == t, found, picked)
    notes = noted.T
    scores = picked.T[:per_owner, :]
    raised = jnp.exp(scores)
    label_weight = jnp.exp(notes[per_owner : 2 * per_owner, :])
    at = 2 * per_owner + 2 * fanout
    label_sum = notes[at : at + 1, :] + notes[at + 1 : at + 2, :]
    share = label_weight / jnp.where(label_sum > 0.0, label_sum, 1.0)
    raised_out[...] = raised
    share_out[...] = share
    notes_out[...] = notes[: notes_out.shape[0], :]
    norm_part = jnp.sum(raised, axis=0, keepdims=True)
    label_part = jnp.sum(share * scores, axis=0, keepdims=True)
    stats = jnp.concatenate(
        [v[:, i * TILE : (i + 1) * TILE] for v in (norm_part, label_part) for i in range(rows // TILE)],
        axis=0,
    )
    stats_out[...] = jnp.broadcast_to(stats[None], stats_out.shape).astype(BF16)


def loss_body(place, stats, target, losses_out, wide, *, chunk):
    rows, fanout = target.shape
    chips, lines, _ = stats.shape
    half = lines // 2
    wide[...] = stats[...].astype(F32).reshape(chips * lines, TILE)
    first = place[3] * chunk
    norm_rows = jnp.zeros((chips, TILE), F32)
    label_rows = jnp.zeros((chips, TILE), F32)
    for i in range(half):
        here = first // TILE == i
        norm_rows = jnp.where(here, wide[pl.ds(i, chips, stride=lines), :], norm_rows)
        label_rows = jnp.where(here, wide[pl.ds(half + i, chips, stride=lines), :], label_rows)
    lane = lax.broadcasted_iota(jnp.int32, (rows, TILE), 1)
    chip = lax.broadcasted_iota(jnp.int32, (rows, chips), 1)
    norm_total = jnp.zeros((rows, 1), F32)
    label_total = jnp.zeros((rows, 1), F32)
    for k in range(fanout):
        slot = target[:, k : k + 1]
        at = ones_of(chip == slot // chunk)
        mine = lane == first % TILE + slot % chunk
        for given, which in ((norm_rows, 0), (label_rows, 1)):
            found = jnp.where(mine, contract(at, given.astype(BF16), 1, 0), 0.0)
            found = jnp.sum(found, axis=1, keepdims=True)
            if which == 0:
                norm_total = norm_total + found
            else:
                label_total = label_total + found
    losses = jnp.broadcast_to(jnp.log(norm_total) - label_total, (rows, TILE))
    losses_out[...] = losses.T[0:1, :]


def pull_body(place, stats, notes, raised, share, own, other, out, wide, *, scale, capacity, fanout, per_owner):
    docs, width = own.shape
    rows = notes.shape[1]
    chunk = CORES * capacity
    chips, lines, _ = stats.shape
    wide[...] = stats[...].astype(F32).reshape(chips * lines, TILE)
    at = 2 * per_owner
    chip = lax.broadcasted_iota(jnp.int32, (chips, fanout * TILE), 0).astype(F32)
    line = lax.broadcasted_iota(jnp.int32, (TILE, fanout * TILE), 0)
    lane = lax.broadcasted_iota(jnp.int32, (1, TILE), 1)
    norms = []
    for i in range(rows // TILE):
        span = slice(i * TILE, (i + 1) * TILE)
        source = jnp.concatenate([notes[at + k : at + k + 1, span] for k in range(fanout)], axis=1)
        start = ((i * TILE + lane) // chunk) * chunk
        slot = jnp.concatenate(
            [
                (start + notes[at + fanout + k : at + fanout + k + 1, span].astype(jnp.int32)) % TILE
                for k in range(fanout)
            ],
            axis=1,
        )
        given = wide[pl.ds(i, chips, stride=lines), :].astype(BF16)
        found = jnp.where(line == slot, contract(given, ones_of(chip == source), 0, 0), 0.0)
        found = jnp.sum(found, axis=0, keepdims=True)
        norms.append(sum(found[:, k * TILE : (k + 1) * TILE] for k in range(fanout)))
    norm_total = jnp.concatenate(norms, axis=1)
    given = (LOSS_SCALE * (raised[...] / norm_total - share[...])).astype(BF16).astype(F32)
    high = at + 2 * fanout
    given = jnp.where(notes[high : high + 1, :] > 0.0, given, 0.0)
    index = lax.broadcasted_iota(jnp.int32, (docs, rows), 0).astype(F32)
    spread = jnp.zeros((docs, rows), F32)
    for m in range(per_owner):
        spread = jnp.where(index == notes[m : m + 1, :], given[m : m + 1, :], spread)
    core = (lax.broadcasted_iota(jnp.int32, (docs, rows), 1) // capacity) % CORES
    mine = core == place[0]
    near = jnp.where(mine, spread, 0.0).astype(BF16)
    far = jnp.where(mine, 0.0, spread).astype(BF16)
    out[...] = (
        (contract(near, own[...], 0, 0) + contract(far, other[...], 0, 0)) * scale
    ).astype(BF16)


def ready_body(arrived, adapter, exact_out, radius_out):
    exact_out[...], radius_out[...] = adapt(arrived[:, : adapter.shape[0]], adapter[...])


def terms_body(place, arrived, exact, radius, pulled, keep_out, give_out, terms):
    width = pulled.shape[1]
    pull = pulled[...].astype(F32)
    projection = jnp.mean(exact[...] * pull, axis=-1, keepdims=True)
    owed = ((pull - exact[...] * projection) / radius[...]).astype(BF16)
    terms[...] = contract(arrived[:, :width], owed, 0, 0)
    lines, _, zs, block, part = keep_out.shape
    core, y, z, x = place[0], place[1], place[2], place[4]
    straight = core == 0
    for whose, out, straight in ((core, keep_out, core == 0), (1 - core, give_out, core != 0)):
        for i in range(lines):
            for l in range(lines):
                row = (y + jnp.where(straight, i, l)) % lines
                column = pl.multiple_of((x + jnp.where(straight, l, i)) % lines * part, TILE)
                for j, far in enumerate(halving(zs)):
                    group = ((z ^ far) * lines + row) * CORES + whose
                    out[i, l, j] = terms[pl.ds(group * block, block), pl.ds(column, part)].astype(BF16)


def grad_body(place, pulled, target, exact, radius, adapter, *rest):
    parts, query_out, adapter_out = rest[:-2], rest[-2], rest[-1]
    size = parts[0].shape[1]
    for q in range(len(parts)):
        steps = (place[4] - q + len(parts)) % len(parts)
        columns = parts[0][...].astype(F32)
        for j in range(1, len(parts)):
            columns = jnp.where(steps == j, parts[j][...].astype(F32), columns)
        adapter_out[:, q * size : (q + 1) * size] = columns.astype(BF16)
    placed = sum(placed_of(target[...], pulled.shape[0]))
    pull_total = contract(placed, pulled[...], 1, 0)
    unit_exact = exact[...]
    projection = jnp.mean(unit_exact * pull_total, axis=-1, keepdims=True)
    adapted_grad = ((pull_total - unit_exact * projection) / radius[...]).astype(BF16)
    query_out[...] = contract(adapted_grad, adapter[...], 1, 1).astype(BF16)


def halving(size):
    order = [0]
    bit = size // 2
    while bit:
        order = order + [one + bit for one in order]
        bit //= 2
    return order


def call(body, name, outs, scratch=(), place=False):
    def run(*args):
        specs = [pl.BlockSpec(memory_space=pltpu.VMEM) for _ in args]
        if place:
            specs[0] = pl.BlockSpec(memory_space=pltpu.SMEM)
        return pl.pallas_call(
            body,
            name=name,
            in_specs=specs,
            out_shape=[jax.ShapeDtypeStruct(shape, dtype) for shape, dtype in outs],
            scratch_shapes=list(scratch),
        )(*args)

    return run


def exchange(rows, chips):
    grouped = rows.reshape(chips, rows.shape[0] // chips, rows.shape[1])
    return lax.all_to_all(grouped, CHIPS, split_axis=0, concat_axis=0, tiled=True).reshape(rows.shape)


def ahead(value, axis, step):
    size = lax.axis_size(axis)
    return lax.ppermute(value, axis, [(i, (i + step) % size) for i in range(size)])


def turned(value, step, first):
    names = ("y", "core", "rep")
    lines = lax.axis_size("y")
    pairs = []
    for y in range(lines):
        for core in range(CORES):
            for x in range(lines):
                along_y = core == first
                to_y = (y + step) % lines if along_y else y
                to_x = x if along_y else (x + step) % lines
                pairs.append(
                    ((y * CORES + core) * lines + x, (to_y * CORES + core) * lines + to_x)
                )
    return lax.ppermute(value, names, pairs)


def added(pieces):
    total = pieces[0].astype(F32)
    for one in pieces[1:]:
        total = total + one.astype(F32)
    return total.astype(BF16)


def halved(value, axis):
    bit = 1
    size = lax.axis_size(axis)
    while value.shape[0] > 1:
        half = value.shape[0] // 2
        got = lax.ppermute(value[half:], axis, [(i, i ^ bit) for i in range(size)])
        value = added([value[:half], got])
        bit *= 2
    return value[0]


def on_device(queries, adapter, doc_table, routes, doc_rows, labels):
    cores, reps = lax.axis_size("core"), lax.axis_size("rep")
    ys, zs = lax.axis_size("y"), lax.axis_size("z")
    owners = cores * reps * ys * zs
    chips = owners // cores
    query_rows, width = queries.shape
    fanout = routes.shape[1]
    per_owner = doc_rows.shape[2]
    docs = doc_table.shape[0]
    capacity = max(2, 2 * query_rows * fanout // owners)
    slots = owners * capacity
    scale = 2.0 / math.sqrt(width)
    flat_rows = doc_rows.transpose(1, 2, 0).reshape(fanout * per_owner, query_rows)
    flat_labels = labels.transpose(1, 2, 0).reshape(fanout * per_owner, query_rows)
    at = {name: lax.axis_index(name) for name in EVERY}
    chip = (at["z"] * ys + at["y"]) * reps + at["rep"]
    place = jnp.stack([at["core"], at["y"], at["z"], chip, at["rep"]]).astype(jnp.int32)

    (own,) = call(unit_body, "unit", [((docs, width), BF16)])(doc_table)
    other = ahead(own, "core", 1)
    outgoing, target = call(
        lambda *refs: send_body(*refs, owners=owners, reps=reps, capacity=capacity),
        "send",
        [((slots, width + TILE), BF16), ((query_rows, fanout), jnp.int32)],
    )(queries, routes.T, flat_rows, flat_labels)
    exact, radius = call(local_body, "local", [((query_rows, width), F32), ((query_rows, 1), F32)])(
        queries, adapter
    )
    arrived = exchange(outgoing, chips)
    arrived, exact, radius = lax.optimization_barrier((arrived, exact, radius))
    lines = 2 * slots // TILE
    noted = -(-(2 * per_owner + 2 * fanout + 2) // 8) * 8
    stats_out, raised, share, notes = call(
        lambda *refs: score_body(
            *refs, scale=scale, capacity=capacity, fanout=fanout, per_owner=per_owner
        ),
        "score",
        [
            ((chips, lines, TILE), BF16),
            ((per_owner, slots), F32),
            ((per_owner, slots), F32),
            ((noted, slots), F32),
        ],
        place=True,
    )(place, arrived, adapter, own, other)
    stats = lax.all_to_all(stats_out, CHIPS, split_axis=0, concat_axis=0, tiled=True)
    held_exact, held_radius = call(ready_body, "ready", [((slots, width), F32), ((slots, 1), F32)])(
        arrived, adapter
    )
    stats, held_exact, held_radius = lax.optimization_barrier((stats, held_exact, held_radius))
    wide = [pltpu.VMEM((chips * lines, TILE), F32)]
    (losses,) = call(
        lambda *refs: loss_body(*refs, chunk=CORES * capacity),
        "loss",
        [((1, query_rows), F32)],
        scratch=wide,
        place=True,
    )(place, stats, target)
    (pull_out,) = call(
        lambda *refs: pull_body(
            *refs, scale=scale, capacity=capacity, fanout=fanout, per_owner=per_owner
        ),
        "pull",
        [((slots, width), BF16)],
        scratch=wide,
        place=True,
    )(place, stats, notes, raised, share, own, other)
    pulled = exchange(pull_out, chips)
    block = width // (cores * ys * zs)
    keep, give = call(
        terms_body,
        "terms",
        [((ys, reps, zs, block, width // reps), BF16)] * 2,
        scratch=[pltpu.VMEM((width, width), F32)],
        place=True,
    )(place, arrived, held_exact, held_radius, pull_out)
    taken = ahead(give, "core", 1)
    pair = [(keep[i].astype(F32) + taken[i].astype(F32)).astype(BF16) for i in range(ys)]
    line = [turned(pair[j], j, 0) for j in range(1, ys)]
    line, losses = lax.optimization_barrier((line, losses))
    line = added(pair[:1] + line)
    plane = added([line[0]] + [turned(line[j], j, 1) for j in range(1, ys)])
    part = halved(plane, "z")
    part = (part.astype(F32) * (1.0 / math.sqrt(query_rows * owners))).astype(BF16)
    got = [part] + [ahead(part, "rep", step) for step in range(1, reps)]
    query_grads, adapter_grad = call(
        grad_body, "grad", [((query_rows, width), BF16), ((block, width), BF16)], place=True
    )(place, pulled, target, exact, radius, adapter, *got)
    return losses.reshape(query_rows), query_grads, adapter_grad


def solution(mesh):
    groups, reps = mesh.devices.shape
    ys = min(4, groups // CORES)
    fine = Mesh(mesh.devices.reshape(groups // (ys * CORES), ys, CORES, reps), EVERY)
    placed = (
        P(EVERY, None),
        P(),
        P(EVERY, None),
        P(EVERY, None),
        P(EVERY, None, None),
        P(EVERY, None, None),
    )
    return jax.shard_map(
        on_device,
        mesh=fine,
        in_specs=placed,
        out_specs=(P(EVERY), P(EVERY, None), P(DOCS, None)),
        check_vma=False,
    )
```

```python
import math

import jax
import jax.numpy as jnp
from jax import lax
from jax.experimental import pallas as pl
from jax.experimental.pallas import tpu as pltpu
from jax.sharding import Mesh
from jax.sharding import PartitionSpec as P

EPSILON = 1e-06
LOSS_SCALE = 128.0
F32 = jnp.float32
BF16 = jnp.bfloat16
TILE = 128
CORES = 2
CHIPS = ("z", "y", "rep")
DOCS = ("z", "y", "core")
EVERY = ("z", "y", "core", "rep")


def contract(left, right, left_dim, right_dim):
    return lax.dot_general(
        left, right, (((left_dim,), (right_dim,)), ((), ())), preferred_element_type=F32
    )


def ones_of(hit):
    return jnp.where(hit, 1.0, 0.0).astype(BF16)


def placed_of(target, slots):
    rows, fanout = target.shape
    index = lax.broadcasted_iota(jnp.int32, (rows, slots), 1)
    return [ones_of(index == target[:, k : k + 1]) for k in range(fanout)]


def by_owner(flat, fanout):
    n = flat.shape[1] // fanout
    return jnp.concatenate([flat[:, k * n : (k + 1) * n] for k in range(fanout)], axis=0)


def unit_body(table, out):
    widened = table[...].astype(F32)
    out[...] = (
        widened / jnp.sqrt(jnp.mean(widened * widened, axis=-1, keepdims=True) + EPSILON)
    ).astype(BF16)


def adapt(rows, adapter):
    adapted = contract(rows, adapter, 1, 0)
    radius = jnp.sqrt(jnp.mean(adapted * adapted, axis=-1, keepdims=True) + EPSILON)
    return adapted / radius, radius


def local_body(queries, adapter, exact_out, radius_out):
    exact_out[...], radius_out[...] = adapt(queries[...], adapter[...])


def send_body(queries, routes, doc_rows, labels, out, target_out, *, owners, reps, capacity):
    fanout, rows = routes.shape
    width = queries.shape[1]
    blank = jnp.zeros((TILE - fanout, rows), F32)
    named_owners = jnp.concatenate([routes[...].astype(F32), blank], axis=0).T[:, :fanout]
    named_owners = named_owners.astype(jnp.int32)
    owner_index = lax.broadcasted_iota(jnp.int32, (rows, owners), 1)
    hits = [jnp.where(owner_index == named_owners[:, k : k + 1], 1.0, 0.0) for k in range(fanout)]
    named = sum(hits).astype(BF16)
    lower = lax.broadcasted_iota(jnp.int32, (rows, rows), 0) > lax.broadcasted_iota(
        jnp.int32, (rows, rows), 1
    )
    earlier = contract(ones_of(lower), named, 1, 0)
    slot = jnp.concatenate(
        [jnp.sum(earlier * hit, axis=1, keepdims=True) for hit in hits], axis=1
    ).astype(jnp.int32)
    owner = named_owners
    rep = owner % reps
    group = owner // reps
    core = group % CORES
    chip = (group // CORES) * reps + rep
    target = (chip * CORES + core) * capacity + slot
    target_out[...] = target
    placed = placed_of(target, owners * capacity)
    out[:, :width] = contract(sum(placed), queries[...], 0, 0).astype(BF16)
    graded = labels[...].astype(F32).T
    label_sum = jnp.sum(jnp.exp(graded), axis=1, keepdims=True)
    high = label_sum.astype(BF16).astype(F32)
    chunk = CORES * capacity
    shared = jnp.concatenate(
        [(target // chunk).astype(F32), (target % chunk).astype(F32), high, label_sum - high], axis=1
    )
    notes = jnp.concatenate(
        [
            by_owner(doc_rows[...].astype(F32).T, fanout),
            by_owner(graded, fanout),
            jnp.concatenate([shared] * fanout, axis=0),
        ],
        axis=1,
    )
    notes = jnp.concatenate(
        [notes, jnp.zeros((fanout * rows, TILE - notes.shape[1]), F32)], axis=1
    ).astype(BF16)
    out[:, width:] = contract(jnp.concatenate(placed, axis=0), notes, 0, 0).astype(BF16)


def score_body(place, arrived, adapter, own, other, stats_out, raised_out, share_out, notes_out, *, scale, capacity, fanout, per_owner):
    width = own.shape[1]
    rows = arrived.shape[0]
    docs = own.shape[0]
    held = adapt(arrived[:, :width], adapter[...])[0].astype(BF16)
    core = (lax.broadcasted_iota(jnp.int32, (rows, docs), 0) // capacity) % CORES
    block = (
        jnp.where(core == place[0], contract(held, own[...], 1, 1), contract(held, other[...], 1, 1))
        * scale
    )
    noted = arrived[:, width:].astype(F32)
    wanted = noted.astype(jnp.int32)
    inner = wanted % TILE
    part = wanted // TILE
    picked = jnp.zeros((rows, TILE), F32)
    for t in range(docs // TILE):
        found = jnp.take_along_axis(block[:, t * TILE : (t + 1) * TILE], inner, axis=1)
        picked = jnp.where(part == t, found, picked)
    notes = noted.T
    scores = picked.T[:per_owner, :]
    raised = jnp.exp(scores)
    label_weight = jnp.exp(notes[per_owner : 2 * per_owner, :])
    at = 2 * per_owner + 2 * fanout
    label_sum = notes[at : at + 1, :] + notes[at + 1 : at + 2, :]
    share = label_weight / jnp.where(label_sum > 0.0, label_sum, 1.0)
    raised_out[...] = raised
    share_out[...] = share
    notes_out[...] = notes[: notes_out.shape[0], :]
    norm_part = jnp.sum(raised, axis=0, keepdims=True)
    label_part = jnp.sum(share * scores, axis=0, keepdims=True)
    stats = jnp.concatenate(
        [v[:, i * TILE : (i + 1) * TILE] for v in (norm_part, label_part) for i in range(rows // TILE)],
        axis=0,
    )
    stats_out[...] = jnp.broadcast_to(stats[None], stats_out.shape).astype(BF16)


def loss_body(place, stats, target, losses_out, wide, *, chunk):
    rows, fanout = target.shape
    chips, lines, _ = stats.shape
    half = lines // 2
    wide[...] = stats[...].astype(F32).reshape(chips * lines, TILE)
    first = place[3] * chunk
    norm_rows = jnp.zeros((chips, TILE), F32)
    label_rows = jnp.zeros((chips, TILE), F32)
    for i in range(half):
        here = first // TILE == i
        norm_rows = jnp.where(here, wide[pl.ds(i, chips, stride=lines), :], norm_rows)
        label_rows = jnp.where(here, wide[pl.ds(half + i, chips, stride=lines), :], label_rows)
    lane = lax.broadcasted_iota(jnp.int32, (rows, TILE), 1)
    chip = lax.broadcasted_iota(jnp.int32, (rows, chips), 1)
    norm_total = jnp.zeros((rows, 1), F32)
    label_total = jnp.zeros((rows, 1), F32)
    for k in range(fanout):
        slot = target[:, k : k + 1]
        at = ones_of(chip == slot // chunk)
        mine = lane == first % TILE + slot % chunk
        for given, which in ((norm_rows, 0), (label_rows, 1)):
            found = jnp.where(mine, contract(at, given.astype(BF16), 1, 0), 0.0)
            found = jnp.sum(found, axis=1, keepdims=True)
            if which == 0:
                norm_total = norm_total + found
            else:
                label_total = label_total + found
    losses = jnp.broadcast_to(jnp.log(norm_total) - label_total, (rows, TILE))
    losses_out[...] = losses.T[0:1, :]


def pull_body(place, stats, notes, raised, share, own, other, arrived, unit, radius, out, keep_out, give_out, wide, terms, *, scale, capacity, fanout, per_owner):
    docs, width = own.shape
    rows = notes.shape[1]
    chunk = CORES * capacity
    chips, lines, _ = stats.shape
    wide[...] = stats[...].astype(F32).reshape(chips * lines, TILE)
    at = 2 * per_owner
    chip = lax.broadcasted_iota(jnp.int32, (chips, fanout * TILE), 0).astype(F32)
    line = lax.broadcasted_iota(jnp.int32, (TILE, fanout * TILE), 0)
    lane = lax.broadcasted_iota(jnp.int32, (1, TILE), 1)
    norms = []
    for i in range(rows // TILE):
        span = slice(i * TILE, (i + 1) * TILE)
        source = jnp.concatenate([notes[at + k : at + k + 1, span] for k in range(fanout)], axis=1)
        start = ((i * TILE + lane) // chunk) * chunk
        slot = jnp.concatenate(
            [
                (start + notes[at + fanout + k : at + fanout + k + 1, span].astype(jnp.int32)) % TILE
                for k in range(fanout)
            ],
            axis=1,
        )
        given = wide[pl.ds(i, chips, stride=lines), :].astype(BF16)
        found = jnp.where(line == slot, contract(given, ones_of(chip == source), 0, 0), 0.0)
        found = jnp.sum(found, axis=0, keepdims=True)
        norms.append(sum(found[:, k * TILE : (k + 1) * TILE] for k in range(fanout)))
    norm_total = jnp.concatenate(norms, axis=1)
    given = (LOSS_SCALE * (raised[...] / norm_total - share[...])).astype(BF16).astype(F32)
    high = at + 2 * fanout
    given = jnp.where(notes[high : high + 1, :] > 0.0, given, 0.0)
    index = lax.broadcasted_iota(jnp.int32, (docs, rows), 0).astype(F32)
    spread = jnp.zeros((docs, rows), F32)
    for m in range(per_owner):
        spread = jnp.where(index == notes[m : m + 1, :], given[m : m + 1, :], spread)
    core = (lax.broadcasted_iota(jnp.int32, (docs, rows), 1) // capacity) % CORES
    mine = core == place[0]
    near = jnp.where(mine, spread, 0.0).astype(BF16)
    far = jnp.where(mine, 0.0, spread).astype(BF16)
    pulled = (
        (contract(near, own[...], 0, 0) + contract(far, other[...], 0, 0)) * scale
    ).astype(BF16)
    out[...] = pulled
    pull = pulled.astype(F32)
    unit_rows = unit[...].astype(F32)
    projection = jnp.mean(unit_rows * pull, axis=-1, keepdims=True)
    owed = ((pull - unit_rows * projection) / radius[...]).astype(BF16)
    terms[...] = contract(arrived[:, :width], owed, 0, 0)
    lines, _, zs, block, part = keep_out.shape
    core, y, z, x = place[0], place[1], place[2], place[4]
    straight = core == 0
    for whose, out, straight in ((core, keep_out, core == 0), (1 - core, give_out, core != 0)):
        for i in range(lines):
            for l in range(lines):
                row = (y + jnp.where(straight, i, l)) % lines
                column = pl.multiple_of((x + jnp.where(straight, l, i)) % lines * part, TILE)
                for j, far in enumerate(halving(zs)):
                    group = ((z ^ far) * lines + row) * CORES + whose
                    out[i, l, j] = terms[pl.ds(group * block, block), pl.ds(column, part)].astype(BF16)


def ready_body(arrived, adapter, unit_out, radius_out):
    exact, radius_out[...] = adapt(arrived[:, : adapter.shape[0]], adapter[...])
    unit_out[...] = exact.astype(BF16)


def grad_body(place, pulled, target, exact, radius, adapter, *rest):
    parts, query_out, adapter_out = rest[:-2], rest[-2], rest[-1]
    size = parts[0].shape[1]
    for q in range(len(parts)):
        steps = (place[4] - q + len(parts)) % len(parts)
        columns = parts[0][...].astype(F32)
        for j in range(1, len(parts)):
            columns = jnp.where(steps == j, parts[j][...].astype(F32), columns)
        adapter_out[:, q * size : (q + 1) * size] = columns.astype(BF16)
    placed = sum(placed_of(target[...], pulled.shape[0]))
    pull_total = contract(placed, pulled[...], 1, 0)
    unit_exact = exact[...]
    projection = jnp.mean(unit_exact * pull_total, axis=-1, keepdims=True)
    adapted_grad = ((pull_total - unit_exact * projection) / radius[...]).astype(BF16)
    query_out[...] = contract(adapted_grad, adapter[...], 1, 1).astype(BF16)


def halving(size):
    order = [0]
    bit = size // 2
    while bit:
        order = order + [one + bit for one in order]
        bit //= 2
    return order


def call(body, name, outs, scratch=(), place=False):
    def run(*args):
        specs = [pl.BlockSpec(memory_space=pltpu.VMEM) for _ in args]
        if place:
            specs[0] = pl.BlockSpec(memory_space=pltpu.SMEM)
        return pl.pallas_call(
            body,
            name=name,
            in_specs=specs,
            out_shape=[jax.ShapeDtypeStruct(shape, dtype) for shape, dtype in outs],
            scratch_shapes=list(scratch),
        )(*args)

    return run


def exchange(rows, chips):
    grouped = rows.reshape(chips, rows.shape[0] // chips, rows.shape[1])
    return lax.all_to_all(grouped, CHIPS, split_axis=0, concat_axis=0, tiled=True).reshape(rows.shape)


def ahead(value, axis, step):
    size = lax.axis_size(axis)
    return lax.ppermute(value, axis, [(i, (i + step) % size) for i in range(size)])


def turned(value, step, first):
    names = ("y", "core", "rep")
    lines = lax.axis_size("y")
    pairs = []
    for y in range(lines):
        for core in range(CORES):
            for x in range(lines):
                along_y = core == first
                to_y = (y + step) % lines if along_y else y
                to_x = x if along_y else (x + step) % lines
                pairs.append(
                    ((y * CORES + core) * lines + x, (to_y * CORES + core) * lines + to_x)
                )
    return lax.ppermute(value, names, pairs)


def added(pieces):
    total = pieces[0].astype(F32)
    for one in pieces[1:]:
        total = total + one.astype(F32)
    return total.astype(BF16)


def halved(value, axis):
    bit = 1
    size = lax.axis_size(axis)
    order = halving(size)
    while value.shape[0] > 4:
        half = value.shape[0] // 2
        got = lax.ppermute(value[half:], axis, [(i, i ^ bit) for i in range(size)])
        value = added([value[:half], got])
        bit *= 2
    got = [
        lax.ppermute(value[j], axis, [(i, i ^ order[j]) for i in range(size)])
        for j in range(1, value.shape[0])
    ]
    return added([value[0]] + got)


def on_device(queries, adapter, doc_table, routes, doc_rows, labels):
    cores, reps = lax.axis_size("core"), lax.axis_size("rep")
    ys, zs = lax.axis_size("y"), lax.axis_size("z")
    owners = cores * reps * ys * zs
    chips = owners // cores
    query_rows, width = queries.shape
    fanout = routes.shape[1]
    per_owner = doc_rows.shape[2]
    docs = doc_table.shape[0]
    capacity = max(2, 2 * query_rows * fanout // owners)
    slots = owners * capacity
    scale = 2.0 / math.sqrt(width)
    flat_rows = doc_rows.transpose(1, 2, 0).reshape(fanout * per_owner, query_rows)
    flat_labels = labels.transpose(1, 2, 0).reshape(fanout * per_owner, query_rows)
    at = {name: lax.axis_index(name) for name in EVERY}
    chip = (at["z"] * ys + at["y"]) * reps + at["rep"]
    place = jnp.stack([at["core"], at["y"], at["z"], chip, at["rep"]]).astype(jnp.int32)

    (own,) = call(unit_body, "unit", [((docs, width), BF16)])(doc_table)
    other = ahead(own, "core", 1)
    outgoing, target = call(
        lambda *refs: send_body(*refs, owners=owners, reps=reps, capacity=capacity),
        "send",
        [((slots, width + TILE), BF16), ((query_rows, fanout), jnp.int32)],
    )(queries, routes.T, flat_rows, flat_labels)
    exact, radius = call(local_body, "local", [((query_rows, width), F32), ((query_rows, 1), F32)])(
        queries, adapter
    )
    arrived = exchange(outgoing, chips)
    arrived, exact, radius = lax.optimization_barrier((arrived, exact, radius))
    lines = 2 * slots // TILE
    noted = -(-(2 * per_owner + 2 * fanout + 2) // 8) * 8
    stats_out, raised, share, notes = call(
        lambda *refs: score_body(
            *refs, scale=scale, capacity=capacity, fanout=fanout, per_owner=per_owner
        ),
        "score",
        [
            ((chips, lines, TILE), BF16),
            ((per_owner, slots), F32),
            ((per_owner, slots), F32),
            ((noted, slots), F32),
        ],
        place=True,
    )(place, arrived, adapter, own, other)
    stats = lax.all_to_all(stats_out, CHIPS, split_axis=0, concat_axis=0, tiled=True)
    held_unit, held_radius = call(ready_body, "ready", [((slots, width), BF16), ((slots, 1), F32)])(
        arrived, adapter
    )
    stats, held_unit, held_radius = lax.optimization_barrier((stats, held_unit, held_radius))
    wide = [pltpu.VMEM((chips * lines, TILE), F32)]
    (losses,) = call(
        lambda *refs: loss_body(*refs, chunk=CORES * capacity),
        "loss",
        [((1, query_rows), F32)],
        scratch=wide,
        place=True,
    )(place, stats, target)
    block = width // (cores * ys * zs)
    pull_out, keep, give = call(
        lambda *refs: pull_body(
            *refs, scale=scale, capacity=capacity, fanout=fanout, per_owner=per_owner
        ),
        "pull",
        [((slots, width), BF16)] + [((ys, reps, zs, block, width // reps), BF16)] * 2,
        scratch=wide + [pltpu.VMEM((width, width), F32)],
        place=True,
    )(place, stats, notes, raised, share, own, other, arrived, held_unit, held_radius)
    pulled = exchange(pull_out, chips)
    taken = ahead(give, "core", 1)
    pair = [(keep[i].astype(F32) + taken[i].astype(F32)).astype(BF16) for i in range(ys)]
    line = [turned(pair[j], j, 0) for j in range(1, ys)]
    line, losses = lax.optimization_barrier((line, losses))
    line = added(pair[:1] + line)
    plane = added([line[0]] + [turned(line[j], j, 1) for j in range(1, ys)])
    part = halved(plane, "z")
    part = (part.astype(F32) * (1.0 / math.sqrt(query_rows * owners))).astype(BF16)
    got = [part] + [ahead(part, "rep", step) for step in range(1, reps)]
    query_grads, adapter_grad = call(
        grad_body, "grad", [((query_rows, width), BF16), ((block, width), BF16)], place=True
    )(place, pulled, target, exact, radius, adapter, *got)
    return losses.reshape(query_rows), query_grads, adapter_grad


def solution(mesh):
    groups, reps = mesh.devices.shape
    ys = min(4, groups // CORES)
    fine = Mesh(mesh.devices.reshape(groups // (ys * CORES), ys, CORES, reps), EVERY)
    placed = (
        P(EVERY, None),
        P(),
        P(EVERY, None),
        P(EVERY, None),
        P(EVERY, None, None),
        P(EVERY, None, None),
    )
    return jax.shard_map(
        on_device,
        mesh=fine,
        in_specs=placed,
        out_specs=(P(EVERY), P(EVERY, None), P(DOCS, None)),
        check_vma=False,
    )
```

```python
import math

import jax
import jax.numpy as jnp
from jax import lax
from jax.experimental import pallas as pl
from jax.experimental.pallas import tpu as pltpu
from jax.sharding import Mesh
from jax.sharding import PartitionSpec as P

EPSILON = 1e-06
LOSS_SCALE = 128.0
F32 = jnp.float32
BF16 = jnp.bfloat16
TILE = 128
CORES = 2
CHIPS = ("z", "y", "rep")
DOCS = ("z", "y", "core")
EVERY = ("z", "y", "core", "rep")


def contract(left, right, left_dim, right_dim):
    return lax.dot_general(
        left, right, (((left_dim,), (right_dim,)), ((), ())), preferred_element_type=F32
    )


def ones_of(hit):
    return jnp.where(hit, 1.0, 0.0).astype(BF16)


def placed_of(target, slots):
    rows, fanout = target.shape
    index = lax.broadcasted_iota(jnp.int32, (rows, slots), 1)
    return [ones_of(index == target[:, k : k + 1]) for k in range(fanout)]


def by_owner(flat, fanout):
    n = flat.shape[1] // fanout
    return jnp.concatenate([flat[:, k * n : (k + 1) * n] for k in range(fanout)], axis=0)


def unit_body(table, out):
    widened = table[...].astype(F32)
    out[...] = (
        widened / jnp.sqrt(jnp.mean(widened * widened, axis=-1, keepdims=True) + EPSILON)
    ).astype(BF16)


def adapt(rows, adapter):
    adapted = contract(rows, adapter, 1, 0)
    radius = jnp.sqrt(jnp.mean(adapted * adapted, axis=-1, keepdims=True) + EPSILON)
    return adapted / radius, radius


def local_body(queries, adapter, exact_out, radius_out):
    exact_out[...], radius_out[...] = adapt(queries[...], adapter[...])


def send_body(queries, routes, doc_rows, labels, out, target_out, *, owners, reps, capacity):
    fanout, rows = routes.shape
    width = queries.shape[1]
    blank = jnp.zeros((TILE - fanout, rows), F32)
    named_owners = jnp.concatenate([routes[...].astype(F32), blank], axis=0).T[:, :fanout]
    named_owners = named_owners.astype(jnp.int32)
    owner_index = lax.broadcasted_iota(jnp.int32, (rows, owners), 1)
    hits = [jnp.where(owner_index == named_owners[:, k : k + 1], 1.0, 0.0) for k in range(fanout)]
    named = sum(hits).astype(BF16)
    lower = lax.broadcasted_iota(jnp.int32, (rows, rows), 0) > lax.broadcasted_iota(
        jnp.int32, (rows, rows), 1
    )
    earlier = contract(ones_of(lower), named, 1, 0)
    slot = jnp.concatenate(
        [jnp.sum(earlier * hit, axis=1, keepdims=True) for hit in hits], axis=1
    ).astype(jnp.int32)
    owner = named_owners
    rep = owner % reps
    group = owner // reps
    core = group % CORES
    chip = (group // CORES) * reps + rep
    target = (chip * CORES + core) * capacity + slot
    target_out[...] = target
    placed = placed_of(target, owners * capacity)
    out[:, :width] = contract(sum(placed), queries[...], 0, 0).astype(BF16)
    graded = labels[...].astype(F32).T
    label_sum = jnp.sum(jnp.exp(graded), axis=1, keepdims=True)
    high = label_sum.astype(BF16).astype(F32)
    chunk = CORES * capacity
    shared = jnp.concatenate(
        [(target // chunk).astype(F32), (target % chunk).astype(F32), high, label_sum - high], axis=1
    )
    notes = jnp.concatenate(
        [
            by_owner(doc_rows[...].astype(F32).T, fanout),
            by_owner(graded, fanout),
            jnp.concatenate([shared] * fanout, axis=0),
        ],
        axis=1,
    )
    notes = jnp.concatenate(
        [notes, jnp.zeros((fanout * rows, TILE - notes.shape[1]), F32)], axis=1
    ).astype(BF16)
    out[:, width:] = contract(jnp.concatenate(placed, axis=0), notes, 0, 0).astype(BF16)


def score_body(place, arrived, adapter, own, other, stats_out, raised_out, share_out, notes_out, *, scale, capacity, fanout, per_owner):
    width = own.shape[1]
    rows = arrived.shape[0]
    docs = own.shape[0]
    held = adapt(arrived[:, :width], adapter[...])[0].astype(BF16)
    core = (lax.broadcasted_iota(jnp.int32, (rows, docs), 0) // capacity) % CORES
    block = (
        jnp.where(core == place[0], contract(held, own[...], 1, 1), contract(held, other[...], 1, 1))
        * scale
    )
    noted = arrived[:, width:].astype(F32)
    wanted = noted.astype(jnp.int32)
    inner = wanted % TILE
    part = wanted // TILE
    picked = jnp.zeros((rows, TILE), F32)
    for t in range(docs // TILE):
        found = jnp.take_along_axis(block[:, t * TILE : (t + 1) * TILE], inner, axis=1)
        picked = jnp.where(part == t, found, picked)
    notes = noted.T
    scores = picked.T[:per_owner, :]
    raised = jnp.exp(scores)
    label_weight = jnp.exp(notes[per_owner : 2 * per_owner, :])
    at = 2 * per_owner + 2 * fanout
    label_sum = notes[at : at + 1, :] + notes[at + 1 : at + 2, :]
    share = label_weight / jnp.where(label_sum > 0.0, label_sum, 1.0)
    raised_out[...] = raised
    share_out[...] = share
    notes_out[...] = notes[: notes_out.shape[0], :]
    norm_part = jnp.sum(raised, axis=0, keepdims=True)
    label_part = jnp.sum(share * scores, axis=0, keepdims=True)
    stats = jnp.concatenate(
        [v[:, i * TILE : (i + 1) * TILE] for v in (norm_part, label_part) for i in range(rows // TILE)],
        axis=0,
    )
    stats_out[...] = jnp.broadcast_to(stats[None], stats_out.shape).astype(BF16)


def loss_body(place, stats, target, losses_out, wide, *, chunk):
    rows, fanout = target.shape
    chips, lines, _ = stats.shape
    half = lines // 2
    wide[...] = stats[...].astype(F32).reshape(chips * lines, TILE)
    first = place[3] * chunk
    norm_rows = jnp.zeros((chips, TILE), F32)
    label_rows = jnp.zeros((chips, TILE), F32)
    for i in range(half):
        here = first // TILE == i
        norm_rows = jnp.where(here, wide[pl.ds(i, chips, stride=lines), :], norm_rows)
        label_rows = jnp.where(here, wide[pl.ds(half + i, chips, stride=lines), :], label_rows)
    lane = lax.broadcasted_iota(jnp.int32, (rows, TILE), 1)
    chip = lax.broadcasted_iota(jnp.int32, (rows, chips), 1)
    norm_total = jnp.zeros((rows, 1), F32)
    label_total = jnp.zeros((rows, 1), F32)
    for k in range(fanout):
        slot = target[:, k : k + 1]
        at = ones_of(chip == slot // chunk)
        mine = lane == first % TILE + slot % chunk
        for given, which in ((norm_rows, 0), (label_rows, 1)):
            found = jnp.where(mine, contract(at, given.astype(BF16), 1, 0), 0.0)
            found = jnp.sum(found, axis=1, keepdims=True)
            if which == 0:
                norm_total = norm_total + found
            else:
                label_total = label_total + found
    losses = jnp.broadcast_to(jnp.log(norm_total) - label_total, (rows, TILE))
    losses_out[...] = losses.T[0:1, :]


def pull_body(place, stats, notes, raised, share, own, other, out, wide, *, scale, capacity, fanout, per_owner):
    docs, width = own.shape
    rows = notes.shape[1]
    chunk = CORES * capacity
    chips, lines, _ = stats.shape
    wide[...] = stats[...].astype(F32).reshape(chips * lines, TILE)
    at = 2 * per_owner
    chip = lax.broadcasted_iota(jnp.int32, (chips, fanout * TILE), 0).astype(F32)
    line = lax.broadcasted_iota(jnp.int32, (TILE, fanout * TILE), 0)
    lane = lax.broadcasted_iota(jnp.int32, (1, TILE), 1)
    norms = []
    for i in range(rows // TILE):
        span = slice(i * TILE, (i + 1) * TILE)
        source = jnp.concatenate([notes[at + k : at + k + 1, span] for k in range(fanout)], axis=1)
        start = ((i * TILE + lane) // chunk) * chunk
        slot = jnp.concatenate(
            [
                (start + notes[at + fanout + k : at + fanout + k + 1, span].astype(jnp.int32)) % TILE
                for k in range(fanout)
            ],
            axis=1,
        )
        given = wide[pl.ds(i, chips, stride=lines), :].astype(BF16)
        found = jnp.where(line == slot, contract(given, ones_of(chip == source), 0, 0), 0.0)
        found = jnp.sum(found, axis=0, keepdims=True)
        norms.append(sum(found[:, k * TILE : (k + 1) * TILE] for k in range(fanout)))
    norm_total = jnp.concatenate(norms, axis=1)
    given = (LOSS_SCALE * (raised[...] / norm_total - share[...])).astype(BF16).astype(F32)
    high = at + 2 * fanout
    given = jnp.where(notes[high : high + 1, :] > 0.0, given, 0.0)
    index = lax.broadcasted_iota(jnp.int32, (docs, rows), 0).astype(F32)
    spread = jnp.zeros((docs, rows), F32)
    for m in range(per_owner):
        spread = jnp.where(index == notes[m : m + 1, :], given[m : m + 1, :], spread)
    core = (lax.broadcasted_iota(jnp.int32, (docs, rows), 1) // capacity) % CORES
    mine = core == place[0]
    near = jnp.where(mine, spread, 0.0).astype(BF16)
    far = jnp.where(mine, 0.0, spread).astype(BF16)
    out[...] = (
        (contract(near, own[...], 0, 0) + contract(far, other[...], 0, 0)) * scale
    ).astype(BF16)


def ready_body(arrived, adapter, unit_out, radius_out):
    exact, radius_out[...] = adapt(arrived[:, : adapter.shape[0]], adapter[...])
    unit_out[...] = exact.astype(BF16)


def terms_body(place, arrived, unit, radius, pulled, keep_out, give_out, terms):
    width = pulled.shape[1]
    pull = pulled[...].astype(F32)
    unit_rows = unit[...].astype(F32)
    projection = jnp.mean(unit_rows * pull, axis=-1, keepdims=True)
    owed = ((pull - unit_rows * projection) / radius[...]).astype(BF16)
    terms[...] = contract(arrived[:, :width], owed, 0, 0)
    lines, _, zs, block, part = keep_out.shape
    core, y, x = place[0], place[1], place[4]
    straight = core == 0
    for whose, out, straight in ((core, keep_out, core == 0), (1 - core, give_out, core != 0)):
        for i in range(lines):
            for l in range(lines):
                row = (y + jnp.where(straight, i, l)) % lines
                column = pl.multiple_of((x + jnp.where(straight, l, i)) % lines * part, TILE)
                for j in range(zs):
                    group = (j * lines + row) * CORES + whose
                    out[i, l, j] = terms[pl.ds(group * block, block), pl.ds(column, part)].astype(BF16)


def grad_body(pulled, target, exact, radius, adapter, query_out):
    placed = sum(placed_of(target[...], pulled.shape[0]))
    pull_total = contract(placed, pulled[...], 1, 0)
    unit_exact = exact[...]
    projection = jnp.mean(unit_exact * pull_total, axis=-1, keepdims=True)
    adapted_grad = ((pull_total - unit_exact * projection) / radius[...]).astype(BF16)
    query_out[...] = contract(adapted_grad, adapter[...], 1, 1).astype(BF16)


def settle_body(parts, adapter_out, *, scale):
    zs, reps = parts.shape[:2]
    size = parts.shape[3]
    for r in range(reps):
        columns = parts[0, r].astype(F32)
        for z in range(1, zs):
            columns = columns + parts[z, r].astype(F32)
        adapter_out[:, r * size : (r + 1) * size] = (columns * scale).astype(BF16)


def call(body, name, outs, scratch=(), place=False):
    def run(*args):
        specs = [pl.BlockSpec(memory_space=pltpu.VMEM) for _ in args]
        if place:
            specs[0] = pl.BlockSpec(memory_space=pltpu.SMEM)
        return pl.pallas_call(
            body,
            name=name,
            in_specs=specs,
            out_shape=[jax.ShapeDtypeStruct(shape, dtype) for shape, dtype in outs],
            scratch_shapes=list(scratch),
        )(*args)

    return run


def exchange(rows, chips):
    grouped = rows.reshape(chips, rows.shape[0] // chips, rows.shape[1])
    return lax.all_to_all(grouped, CHIPS, split_axis=0, concat_axis=0, tiled=True).reshape(rows.shape)


def ahead(value, axis, step):
    size = lax.axis_size(axis)
    return lax.ppermute(value, axis, [(i, (i + step) % size) for i in range(size)])


def turned(value, step, first):
    names = ("y", "core", "rep")
    lines = lax.axis_size("y")
    pairs = []
    for y in range(lines):
        for core in range(CORES):
            for x in range(lines):
                along_y = core == first
                to_y = (y + step) % lines if along_y else y
                to_x = x if along_y else (x + step) % lines
                pairs.append(
                    ((y * CORES + core) * lines + x, (to_y * CORES + core) * lines + to_x)
                )
    return lax.ppermute(value, names, pairs)


def added(pieces):
    total = pieces[0].astype(F32)
    for one in pieces[1:]:
        total = total + one.astype(F32)
    return total.astype(BF16)


def on_device(queries, adapter, doc_table, routes, doc_rows, labels):
    cores, reps = lax.axis_size("core"), lax.axis_size("rep")
    ys, zs = lax.axis_size("y"), lax.axis_size("z")
    owners = cores * reps * ys * zs
    chips = owners // cores
    query_rows, width = queries.shape
    fanout = routes.shape[1]
    per_owner = doc_rows.shape[2]
    docs = doc_table.shape[0]
    capacity = max(2, 2 * query_rows * fanout // owners)
    slots = owners * capacity
    scale = 2.0 / math.sqrt(width)
    flat_rows = doc_rows.transpose(1, 2, 0).reshape(fanout * per_owner, query_rows)
    flat_labels = labels.transpose(1, 2, 0).reshape(fanout * per_owner, query_rows)
    at = {name: lax.axis_index(name) for name in EVERY}
    chip = (at["z"] * ys + at["y"]) * reps + at["rep"]
    place = jnp.stack([at["core"], at["y"], at["z"], chip, at["rep"]]).astype(jnp.int32)

    (own,) = call(unit_body, "unit", [((docs, width), BF16)])(doc_table)
    other = ahead(own, "core", 1)
    outgoing, target = call(
        lambda *refs: send_body(*refs, owners=owners, reps=reps, capacity=capacity),
        "send",
        [((slots, width + TILE), BF16), ((query_rows, fanout), jnp.int32)],
    )(queries, routes.T, flat_rows, flat_labels)
    exact, radius = call(local_body, "local", [((query_rows, width), F32), ((query_rows, 1), F32)])(
        queries, adapter
    )
    arrived = exchange(outgoing, chips)
    arrived, exact, radius = lax.optimization_barrier((arrived, exact, radius))
    lines = 2 * slots // TILE
    noted = -(-(2 * per_owner + 2 * fanout + 2) // 8) * 8
    stats_out, raised, share, notes = call(
        lambda *refs: score_body(
            *refs, scale=scale, capacity=capacity, fanout=fanout, per_owner=per_owner
        ),
        "score",
        [
            ((chips, lines, TILE), BF16),
            ((per_owner, slots), F32),
            ((per_owner, slots), F32),
            ((noted, slots), F32),
        ],
        place=True,
    )(place, arrived, adapter, own, other)
    stats = lax.all_to_all(stats_out, CHIPS, split_axis=0, concat_axis=0, tiled=True)
    held_unit, held_radius = call(ready_body, "ready", [((slots, width), BF16), ((slots, 1), F32)])(
        arrived, adapter
    )
    stats, held_unit, held_radius = lax.optimization_barrier((stats, held_unit, held_radius))
    wide = [pltpu.VMEM((chips * lines, TILE), F32)]
    (losses,) = call(
        lambda *refs: loss_body(*refs, chunk=CORES * capacity),
        "loss",
        [((1, query_rows), F32)],
        scratch=wide,
        place=True,
    )(place, stats, target)
    (pull_out,) = call(
        lambda *refs: pull_body(
            *refs, scale=scale, capacity=capacity, fanout=fanout, per_owner=per_owner
        ),
        "pull",
        [((slots, width), BF16)],
        scratch=wide,
        place=True,
    )(place, stats, notes, raised, share, own, other)
    pulled = exchange(pull_out, chips)
    block = width // (cores * ys * zs)
    keep, give = call(
        terms_body,
        "terms",
        [((ys, reps, zs, block, width // reps), BF16)] * 2,
        scratch=[pltpu.VMEM((width, width), F32)],
        place=True,
    )(place, arrived, held_unit, held_radius, pull_out)
    taken = ahead(give, "core", 1)
    pair = [(keep[i].astype(F32) + taken[i].astype(F32)).astype(BF16) for i in range(ys)]
    line = [turned(pair[j], j, 0) for j in range(1, ys)]
    line, losses = lax.optimization_barrier((line, losses))
    line = added(pair[:1] + line)
    plane = added([line[0]] + [turned(line[j], j, 1) for j in range(1, ys)])
    plane, pulled = lax.optimization_barrier((plane, pulled))
    sent = jnp.broadcast_to(plane[:, None], (zs, reps) + plane.shape[1:])
    sent = sent.reshape((zs * reps,) + plane.shape[1:])
    settled = lax.all_to_all(sent, ("z", "rep"), split_axis=0, concat_axis=0, tiled=True)
    (query_grads,) = call(grad_body, "grad", [((query_rows, width), BF16)])(
        pulled, target, exact, radius, adapter
    )
    (adapter_grad,) = call(
        lambda *refs: settle_body(*refs, scale=1.0 / math.sqrt(query_rows * owners)),
        "settle",
        [((block, width), BF16)],
    )(settled.reshape((zs, reps) + plane.shape[1:]))
    return losses.reshape(query_rows), query_grads, adapter_grad


def solution(mesh):
    groups, reps = mesh.devices.shape
    ys = min(4, groups // CORES)
    fine = Mesh(mesh.devices.reshape(groups // (ys * CORES), ys, CORES, reps), EVERY)
    placed = (
        P(EVERY, None),
        P(),
        P(EVERY, None),
        P(EVERY, None),
        P(EVERY, None, None),
        P(EVERY, None, None),
    )
    return jax.shard_map(
        on_device,
        mesh=fine,
        in_specs=placed,
        out_specs=(P(EVERY), P(EVERY, None), P(DOCS, None)),
        check_vma=False,
    )
```

```python
import math

import jax
import jax.numpy as jnp
from jax import lax
from jax.experimental import pallas as pl
from jax.experimental.pallas import tpu as pltpu
from jax.sharding import Mesh
from jax.sharding import PartitionSpec as P

EPSILON = 1e-06
LOSS_SCALE = 128.0
F32 = jnp.float32
BF16 = jnp.bfloat16
TILE = 128
CORES = 2
CHIPS = ("z", "y", "rep")
DOCS = ("z", "y", "core")
EVERY = ("z", "y", "core", "rep")


def contract(left, right, left_dim, right_dim):
    return lax.dot_general(
        left, right, (((left_dim,), (right_dim,)), ((), ())), preferred_element_type=F32
    )


def ones_of(hit):
    return jnp.where(hit, 1.0, 0.0).astype(BF16)


def placed_of(target, slots):
    rows, fanout = target.shape
    index = lax.broadcasted_iota(jnp.int32, (rows, slots), 1)
    return [ones_of(index == target[:, k : k + 1]) for k in range(fanout)]


def by_owner(flat, fanout):
    n = flat.shape[1] // fanout
    return jnp.concatenate([flat[:, k * n : (k + 1) * n] for k in range(fanout)], axis=0)


def unit_body(table, out):
    widened = table[...].astype(F32)
    out[...] = (
        widened / jnp.sqrt(jnp.mean(widened * widened, axis=-1, keepdims=True) + EPSILON)
    ).astype(BF16)


def adapt(rows, adapter):
    adapted = contract(rows, adapter, 1, 0)
    radius = jnp.sqrt(jnp.mean(adapted * adapted, axis=-1, keepdims=True) + EPSILON)
    return adapted / radius, radius


def local_body(queries, adapter, exact_out, radius_out):
    exact_out[...], radius_out[...] = adapt(queries[...], adapter[...])


def send_body(queries, routes, doc_rows, labels, out, target_out, *, owners, reps, capacity):
    fanout, rows = routes.shape
    width = queries.shape[1]
    blank = jnp.zeros((TILE - fanout, rows), F32)
    named_owners = jnp.concatenate([routes[...].astype(F32), blank], axis=0).T[:, :fanout]
    named_owners = named_owners.astype(jnp.int32)
    owner_index = lax.broadcasted_iota(jnp.int32, (rows, owners), 1)
    hits = [jnp.where(owner_index == named_owners[:, k : k + 1], 1.0, 0.0) for k in range(fanout)]
    named = sum(hits).astype(BF16)
    lower = lax.broadcasted_iota(jnp.int32, (rows, rows), 0) > lax.broadcasted_iota(
        jnp.int32, (rows, rows), 1
    )
    earlier = contract(ones_of(lower), named, 1, 0)
    slot = jnp.concatenate(
        [jnp.sum(earlier * hit, axis=1, keepdims=True) for hit in hits], axis=1
    ).astype(jnp.int32)
    owner = named_owners
    rep = owner % reps
    group = owner // reps
    core = group % CORES
    chip = (group // CORES) * reps + rep
    target = (chip * CORES + core) * capacity + slot
    target_out[...] = target
    placed = placed_of(target, owners * capacity)
    out[:, :width] = contract(sum(placed), queries[...], 0, 0).astype(BF16)
    graded = labels[...].astype(F32).T
    label_sum = jnp.sum(jnp.exp(graded), axis=1, keepdims=True)
    high = label_sum.astype(BF16).astype(F32)
    chunk = CORES * capacity
    shared = jnp.concatenate(
        [(target // chunk).astype(F32), (target % chunk).astype(F32), high, label_sum - high], axis=1
    )
    notes = jnp.concatenate(
        [
            by_owner(doc_rows[...].astype(F32).T, fanout),
            by_owner(graded, fanout),
            jnp.concatenate([shared] * fanout, axis=0),
        ],
        axis=1,
    )
    notes = jnp.concatenate(
        [notes, jnp.zeros((fanout * rows, TILE - notes.shape[1]), F32)], axis=1
    ).astype(BF16)
    out[:, width:] = contract(jnp.concatenate(placed, axis=0), notes, 0, 0).astype(BF16)


def score_body(place, arrived, adapter, own, other, stats_out, raised_out, share_out, notes_out, *, scale, capacity, fanout, per_owner):
    width = own.shape[1]
    rows = arrived.shape[0]
    docs = own.shape[0]
    held = adapt(arrived[:, :width], adapter[...])[0].astype(BF16)
    core = (lax.broadcasted_iota(jnp.int32, (rows, docs), 0) // capacity) % CORES
    block = (
        jnp.where(core == place[0], contract(held, own[...], 1, 1), contract(held, other[...], 1, 1))
        * scale
    )
    noted = arrived[:, width:].astype(F32)
    wanted = noted.astype(jnp.int32)
    inner = wanted % TILE
    part = wanted // TILE
    picked = jnp.zeros((rows, TILE), F32)
    for t in range(docs // TILE):
        found = jnp.take_along_axis(block[:, t * TILE : (t + 1) * TILE], inner, axis=1)
        picked = jnp.where(part == t, found, picked)
    notes = noted.T
    scores = picked.T[:per_owner, :]
    raised = jnp.exp(scores)
    label_weight = jnp.exp(notes[per_owner : 2 * per_owner, :])
    at = 2 * per_owner + 2 * fanout
    label_sum = notes[at : at + 1, :] + notes[at + 1 : at + 2, :]
    share = label_weight / jnp.where(label_sum > 0.0, label_sum, 1.0)
    raised_out[...] = raised
    share_out[...] = share
    notes_out[...] = notes[: notes_out.shape[0], :]
    norm_part = jnp.sum(raised, axis=0, keepdims=True)
    label_part = jnp.sum(share * scores, axis=0, keepdims=True)
    stats = jnp.concatenate(
        [v[:, i * TILE : (i + 1) * TILE] for v in (norm_part, label_part) for i in range(rows // TILE)],
        axis=0,
    )
    stats_out[...] = jnp.broadcast_to(stats[None], stats_out.shape).astype(BF16)


def loss_body(place, stats, target, losses_out, wide, *, chunk):
    rows, fanout = target.shape
    chips, lines, _ = stats.shape
    half = lines // 2
    wide[...] = stats[...].astype(F32).reshape(chips * lines, TILE)
    first = place[3] * chunk
    norm_rows = jnp.zeros((chips, TILE), F32)
    label_rows = jnp.zeros((chips, TILE), F32)
    for i in range(half):
        here = first // TILE == i
        norm_rows = jnp.where(here, wide[pl.ds(i, chips, stride=lines), :], norm_rows)
        label_rows = jnp.where(here, wide[pl.ds(half + i, chips, stride=lines), :], label_rows)
    lane = lax.broadcasted_iota(jnp.int32, (rows, TILE), 1)
    chip = lax.broadcasted_iota(jnp.int32, (rows, chips), 1)
    norm_total = jnp.zeros((rows, 1), F32)
    label_total = jnp.zeros((rows, 1), F32)
    for k in range(fanout):
        slot = target[:, k : k + 1]
        at = ones_of(chip == slot // chunk)
        mine = lane == first % TILE + slot % chunk
        for given, which in ((norm_rows, 0), (label_rows, 1)):
            found = jnp.where(mine, contract(at, given.astype(BF16), 1, 0), 0.0)
            found = jnp.sum(found, axis=1, keepdims=True)
            if which == 0:
                norm_total = norm_total + found
            else:
                label_total = label_total + found
    losses = jnp.broadcast_to(jnp.log(norm_total) - label_total, (rows, TILE))
    losses_out[...] = losses.T[0:1, :]


def pull_body(place, stats, notes, raised, share, own, other, out, wide, *, scale, capacity, fanout, per_owner):
    docs, width = own.shape
    rows = notes.shape[1]
    chunk = CORES * capacity
    chips, lines, _ = stats.shape
    wide[...] = stats[...].astype(F32).reshape(chips * lines, TILE)
    at = 2 * per_owner
    chip = lax.broadcasted_iota(jnp.int32, (chips, fanout * TILE), 0).astype(F32)
    line = lax.broadcasted_iota(jnp.int32, (TILE, fanout * TILE), 0)
    lane = lax.broadcasted_iota(jnp.int32, (1, TILE), 1)
    norms = []
    for i in range(rows // TILE):
        span = slice(i * TILE, (i + 1) * TILE)
        source = jnp.concatenate([notes[at + k : at + k + 1, span] for k in range(fanout)], axis=1)
        start = ((i * TILE + lane) // chunk) * chunk
        slot = jnp.concatenate(
            [
                (start + notes[at + fanout + k : at + fanout + k + 1, span].astype(jnp.int32)) % TILE
                for k in range(fanout)
            ],
            axis=1,
        )
        given = wide[pl.ds(i, chips, stride=lines), :].astype(BF16)
        found = jnp.where(line == slot, contract(given, ones_of(chip == source), 0, 0), 0.0)
        found = jnp.sum(found, axis=0, keepdims=True)
        norms.append(sum(found[:, k * TILE : (k + 1) * TILE] for k in range(fanout)))
    norm_total = jnp.concatenate(norms, axis=1)
    high = at + 2 * fanout
    spread = LOSS_SCALE * (raised[...] / norm_total - share[...])
    spread = jnp.where(notes[high : high + 1, :] > 0.0, spread, 0.0)
    core = (lax.broadcasted_iota(jnp.int32, (docs, rows), 1) // capacity) % CORES
    mine = core == place[0]
    near = jnp.where(mine, spread, 0.0).astype(BF16)
    far = jnp.where(mine, 0.0, spread).astype(BF16)
    out[...] = (
        (contract(near, own[...], 0, 0) + contract(far, other[...], 0, 0)) * scale
    ).astype(BF16)


def ready_body(arrived, notes, raised, share, adapter, unit_out, radius_out, raised_out, share_out):
    exact, radius_out[...] = adapt(arrived[:, : adapter.shape[0]], adapter[...])
    unit_out[...] = exact.astype(BF16)
    index = lax.broadcasted_iota(jnp.int32, raised_out.shape, 0).astype(F32)
    raised_spread = jnp.zeros(raised_out.shape, F32)
    share_spread = jnp.zeros(raised_out.shape, F32)
    for m in range(raised.shape[0]):
        here = index == notes[m : m + 1, :]
        raised_spread = jnp.where(here, raised[m : m + 1, :], raised_spread)
        share_spread = jnp.where(here, share[m : m + 1, :], share_spread)
    raised_out[...] = raised_spread
    share_out[...] = share_spread


def terms_body(place, arrived, unit, radius, pulled, keep_out, give_out, terms):
    width = pulled.shape[1]
    pull = pulled[...].astype(F32)
    unit_rows = unit[...].astype(F32)
    projection = jnp.mean(unit_rows * pull, axis=-1, keepdims=True)
    owed = ((pull - unit_rows * projection) / radius[...]).astype(BF16)
    terms[...] = contract(arrived[:, :width], owed, 0, 0)
    lines, _, zs, block, part = keep_out.shape
    core, y, x = place[0], place[1], place[4]
    straight = core == 0
    for whose, out, straight in ((core, keep_out, core == 0), (1 - core, give_out, core != 0)):
        for i in range(lines):
            for l in range(lines):
                row = (y + jnp.where(straight, i, l)) % lines
                column = pl.multiple_of((x + jnp.where(straight, l, i)) % lines * part, TILE)
                for j in range(zs):
                    group = (j * lines + row) * CORES + whose
                    out[i, l, j] = terms[pl.ds(group * block, block), pl.ds(column, part)].astype(BF16)


def grad_body(pulled, target, exact, radius, adapter, query_out):
    placed = sum(placed_of(target[...], pulled.shape[0]))
    pull_total = contract(placed, pulled[...], 1, 0)
    unit_exact = exact[...]
    projection = jnp.mean(unit_exact * pull_total, axis=-1, keepdims=True)
    adapted_grad = ((pull_total - unit_exact * projection) / radius[...]).astype(BF16)
    query_out[...] = contract(adapted_grad, adapter[...], 1, 1).astype(BF16)


def join_body(*refs):
    pieces, out = refs[:-1], refs[-1]
    total = pieces[0][...].astype(F32)
    for one in pieces[1:]:
        total = total + one[...].astype(F32)
    total = total.astype(BF16)
    for r in range(out.shape[1]):
        out[:, r] = total


def settle_body(parts, adapter_out, *, scale):
    zs, reps = parts.shape[:2]
    size = parts.shape[3]
    for r in range(reps):
        columns = parts[0, r].astype(F32)
        for z in range(1, zs):
            columns = columns + parts[z, r].astype(F32)
        adapter_out[:, r * size : (r + 1) * size] = (columns * scale).astype(BF16)


def call(body, name, outs, scratch=(), place=False, limit=None):
    def run(*args):
        specs = [pl.BlockSpec(memory_space=pltpu.VMEM) for _ in args]
        if place:
            specs[0] = pl.BlockSpec(memory_space=pltpu.SMEM)
        return pl.pallas_call(
            body,
            name=name,
            in_specs=specs,
            out_shape=[jax.ShapeDtypeStruct(shape, dtype) for shape, dtype in outs],
            scratch_shapes=list(scratch),
            compiler_params=pltpu.CompilerParams(vmem_limit_bytes=limit),
        )(*args)

    return run


def exchange(rows, chips):
    grouped = rows.reshape(chips, rows.shape[0] // chips, rows.shape[1])
    return lax.all_to_all(grouped, CHIPS, split_axis=0, concat_axis=0, tiled=True).reshape(rows.shape)


def ahead(value, axis, step):
    size = lax.axis_size(axis)
    return lax.ppermute(value, axis, [(i, (i + step) % size) for i in range(size)])


def turned(value, step, first):
    names = ("y", "core", "rep")
    lines = lax.axis_size("y")
    pairs = []
    for y in range(lines):
        for core in range(CORES):
            for x in range(lines):
                along_y = core == first
                to_y = (y + step) % lines if along_y else y
                to_x = x if along_y else (x + step) % lines
                pairs.append(
                    ((y * CORES + core) * lines + x, (to_y * CORES + core) * lines + to_x)
                )
    return lax.ppermute(value, names, pairs)


def added(pieces):
    total = pieces[0].astype(F32)
    for one in pieces[1:]:
        total = total + one.astype(F32)
    return total.astype(BF16)


def on_device(queries, adapter, doc_table, routes, doc_rows, labels):
    cores, reps = lax.axis_size("core"), lax.axis_size("rep")
    ys, zs = lax.axis_size("y"), lax.axis_size("z")
    owners = cores * reps * ys * zs
    chips = owners // cores
    query_rows, width = queries.shape
    fanout = routes.shape[1]
    per_owner = doc_rows.shape[2]
    docs = doc_table.shape[0]
    capacity = max(2, 2 * query_rows * fanout // owners)
    slots = owners * capacity
    scale = 2.0 / math.sqrt(width)
    flat_rows = doc_rows.transpose(1, 2, 0).reshape(fanout * per_owner, query_rows)
    flat_labels = labels.transpose(1, 2, 0).reshape(fanout * per_owner, query_rows)
    at = {name: lax.axis_index(name) for name in EVERY}
    chip = (at["z"] * ys + at["y"]) * reps + at["rep"]
    place = jnp.stack([at["core"], at["y"], at["z"], chip, at["rep"]]).astype(jnp.int32)

    (own,) = call(unit_body, "unit", [((docs, width), BF16)])(doc_table)
    other = ahead(own, "core", 1)
    outgoing, target = call(
        lambda *refs: send_body(*refs, owners=owners, reps=reps, capacity=capacity),
        "send",
        [((slots, width + TILE), BF16), ((query_rows, fanout), jnp.int32)],
    )(queries, routes.T, flat_rows, flat_labels)
    exact, radius = call(local_body, "local", [((query_rows, width), F32), ((query_rows, 1), F32)])(
        queries, adapter
    )
    arrived = exchange(outgoing, chips)
    arrived, exact, radius = lax.optimization_barrier((arrived, exact, radius))
    lines = 2 * slots // TILE
    noted = -(-(2 * per_owner + 2 * fanout + 2) // 8) * 8
    stats_out, raised, share, notes = call(
        lambda *refs: score_body(
            *refs, scale=scale, capacity=capacity, fanout=fanout, per_owner=per_owner
        ),
        "score",
        [
            ((chips, lines, TILE), BF16),
            ((per_owner, slots), F32),
            ((per_owner, slots), F32),
            ((noted, slots), F32),
        ],
        place=True,
    )(place, arrived, adapter, own, other)
    stats = lax.all_to_all(stats_out, CHIPS, split_axis=0, concat_axis=0, tiled=True)
    ready = call(
        ready_body,
        "ready",
        [((slots, width), BF16), ((slots, 1), F32), ((docs, slots), F32), ((docs, slots), F32)],
    )(arrived, notes, raised, share, adapter)
    stats, ready = lax.optimization_barrier((stats, ready))
    held_unit, held_radius, raised, share = ready
    wide = [pltpu.VMEM((chips * lines, TILE), F32)]
    (losses,) = call(
        lambda *refs: loss_body(*refs, chunk=CORES * capacity),
        "loss",
        [((1, query_rows), F32)],
        scratch=wide,
        place=True,
    )(place, stats, target)
    (pull_out,) = call(
        lambda *refs: pull_body(
            *refs, scale=scale, capacity=capacity, fanout=fanout, per_owner=per_owner
        ),
        "pull",
        [((slots, width), BF16)],
        scratch=wide,
        place=True,
    )(place, stats, notes, raised, share, own, other)
    pulled = exchange(pull_out, chips)
    block = width // (cores * ys * zs)
    keep, give = call(
        terms_body,
        "terms",
        [((ys, reps, zs, block, width // reps), BF16)] * 2,
        scratch=[pltpu.VMEM((width, width), F32)],
        place=True,
    )(place, arrived, held_unit, held_radius, pull_out)
    taken = ahead(give, "core", 1)
    pair = [(keep[i].astype(F32) + taken[i].astype(F32)).astype(BF16) for i in range(ys)]
    line = [turned(pair[j], j, 0) for j in range(1, ys)]
    line, losses = lax.optimization_barrier((line, losses))
    line = added(pair[:1] + line)
    plane = [line[0]] + [turned(line[j], j, 1) for j in range(1, ys)]
    piece = line.shape[2:]
    (sent,) = call(join_body, "join", [((zs, reps) + piece, BF16)])(*plane)
    sent = sent.reshape((zs * reps,) + piece)
    sent, pulled = lax.optimization_barrier((sent, pulled))
    settled = lax.all_to_all(sent, ("z", "rep"), split_axis=0, concat_axis=0, tiled=True)
    (query_grads,) = call(grad_body, "grad", [((query_rows, width), BF16)])(
        pulled, target, exact, radius, adapter
    )
    (adapter_grad,) = call(
        lambda *refs: settle_body(*refs, scale=1.0 / math.sqrt(query_rows * owners)),
        "settle",
        [((block, width), BF16)],
        limit=16 * 2**20,
    )(settled.reshape((zs, reps) + piece))
    return losses.reshape(query_rows), query_grads, adapter_grad


def solution(mesh):
    groups, reps = mesh.devices.shape
    ys = min(4, groups // CORES)
    fine = Mesh(mesh.devices.reshape(groups // (ys * CORES), ys, CORES, reps), EVERY)
    placed = (
        P(EVERY, None),
        P(),
        P(EVERY, None),
        P(EVERY, None),
        P(EVERY, None, None),
        P(EVERY, None, None),
    )
    return jax.shard_map(
        on_device,
        mesh=fine,
        in_specs=placed,
        out_specs=(P(EVERY), P(EVERY, None), P(DOCS, None)),
        check_vma=False,
    )
```

```python
import math

import jax
import jax.numpy as jnp
from jax import lax
from jax.experimental import pallas as pl
from jax.experimental.pallas import tpu as pltpu
from jax.sharding import Mesh
from jax.sharding import PartitionSpec as P

EPSILON = 1e-06
LOSS_SCALE = 128.0
F32 = jnp.float32
BF16 = jnp.bfloat16
TILE = 128
CORES = 2
CHIPS = ("z", "y", "rep")
DOCS = ("z", "y", "core")
EVERY = ("z", "y", "core", "rep")


def contract(left, right, left_dim, right_dim):
    return lax.dot_general(
        left, right, (((left_dim,), (right_dim,)), ((), ())), preferred_element_type=F32
    )


def ones_of(hit):
    return jnp.where(hit, 1.0, 0.0).astype(BF16)


def placed_of(target, slots):
    rows, fanout = target.shape
    index = lax.broadcasted_iota(jnp.int32, (rows, slots), 1)
    return [ones_of(index == target[:, k : k + 1]) for k in range(fanout)]


def by_owner(flat, fanout):
    n = flat.shape[1] // fanout
    return jnp.concatenate([flat[:, k * n : (k + 1) * n] for k in range(fanout)], axis=0)


def unit_body(table, out):
    widened = table[...].astype(F32)
    out[...] = (
        widened / jnp.sqrt(jnp.mean(widened * widened, axis=-1, keepdims=True) + EPSILON)
    ).astype(BF16)


def adapt(rows, adapter):
    adapted = contract(rows, adapter, 1, 0)
    radius = jnp.sqrt(jnp.mean(adapted * adapted, axis=-1, keepdims=True) + EPSILON)
    return adapted / radius, radius


def local_body(queries, adapter, exact_out, radius_out):
    exact_out[...], radius_out[...] = adapt(queries[...], adapter[...])


def send_body(queries, routes, doc_rows, labels, out, target_out, *, owners, reps, capacity):
    fanout, rows = routes.shape
    width = queries.shape[1]
    blank = jnp.zeros((TILE - fanout, rows), F32)
    named_owners = jnp.concatenate([routes[...].astype(F32), blank], axis=0).T[:, :fanout]
    named_owners = named_owners.astype(jnp.int32)
    owner_index = lax.broadcasted_iota(jnp.int32, (rows, owners), 1)
    hits = [jnp.where(owner_index == named_owners[:, k : k + 1], 1.0, 0.0) for k in range(fanout)]
    named = sum(hits).astype(BF16)
    lower = lax.broadcasted_iota(jnp.int32, (rows, rows), 0) > lax.broadcasted_iota(
        jnp.int32, (rows, rows), 1
    )
    earlier = contract(ones_of(lower), named, 1, 0)
    slot = jnp.concatenate(
        [jnp.sum(earlier * hit, axis=1, keepdims=True) for hit in hits], axis=1
    ).astype(jnp.int32)
    owner = named_owners
    rep = owner % reps
    group = owner // reps
    core = group % CORES
    chip = (group // CORES) * reps + rep
    target = (chip * CORES + core) * capacity + slot
    target_out[...] = target
    placed = placed_of(target, owners * capacity)
    out[:, :width] = contract(sum(placed), queries[...], 0, 0).astype(BF16)
    graded = labels[...].astype(F32).T
    label_sum = jnp.sum(jnp.exp(graded), axis=1, keepdims=True)
    high = label_sum.astype(BF16).astype(F32)
    chunk = CORES * capacity
    shared = jnp.concatenate(
        [(target // chunk).astype(F32), (target % chunk).astype(F32), high, label_sum - high], axis=1
    )
    notes = jnp.concatenate(
        [
            by_owner(doc_rows[...].astype(F32).T, fanout),
            by_owner(graded, fanout),
            jnp.concatenate([shared] * fanout, axis=0),
        ],
        axis=1,
    )
    notes = jnp.concatenate(
        [notes, jnp.zeros((fanout * rows, TILE - notes.shape[1]), F32)], axis=1
    ).astype(BF16)
    out[:, width:] = contract(jnp.concatenate(placed, axis=0), notes, 0, 0).astype(BF16)


def score_body(place, arrived, adapter, own, other, stats_out, book_out, *, scale, capacity, fanout, per_owner):
    width = own.shape[1]
    rows = arrived.shape[0]
    docs = own.shape[0]
    held = adapt(arrived[:, :width], adapter[...])[0].astype(BF16)
    core = (lax.broadcasted_iota(jnp.int32, (rows, docs), 0) // capacity) % CORES
    block = (
        jnp.where(core == place[0], contract(held, own[...], 1, 1), contract(held, other[...], 1, 1))
        * scale
    )
    noted = arrived[:, width:].astype(F32)
    wanted = noted.astype(jnp.int32)
    inner = wanted % TILE
    part = wanted // TILE
    picked = jnp.zeros((rows, TILE), F32)
    for t in range(docs // TILE):
        found = jnp.take_along_axis(block[:, t * TILE : (t + 1) * TILE], inner, axis=1)
        picked = jnp.where(part == t, found, picked)
    notes = noted.T
    scores = picked.T[:per_owner, :]
    raised = jnp.exp(scores)
    label_weight = jnp.exp(notes[per_owner : 2 * per_owner, :])
    at = 2 * per_owner + 2 * fanout
    label_sum = notes[at : at + 1, :] + notes[at + 1 : at + 2, :]
    share = label_weight / jnp.where(label_sum > 0.0, label_sum, 1.0)
    noted_rows = book_out.shape[0] - 2 * per_owner
    book_out[...] = jnp.concatenate([notes[:noted_rows, :], raised, share], axis=0)
    norm_part = jnp.sum(raised, axis=0, keepdims=True)
    label_part = jnp.sum(share * scores, axis=0, keepdims=True)
    stats = jnp.concatenate(
        [v[:, i * TILE : (i + 1) * TILE] for v in (norm_part, label_part) for i in range(rows // TILE)],
        axis=0,
    )
    stats_out[...] = jnp.broadcast_to(stats[None], stats_out.shape).astype(BF16)


def loss_body(place, stats, target, losses_out, wide, *, chunk):
    rows, fanout = target.shape
    chips, lines, _ = stats.shape
    half = lines // 2
    wide[...] = stats[...].astype(F32).reshape(chips * lines, TILE)
    first = place[3] * chunk
    norm_rows = jnp.zeros((chips, TILE), F32)
    label_rows = jnp.zeros((chips, TILE), F32)
    for i in range(half):
        here = first // TILE == i
        norm_rows = jnp.where(here, wide[pl.ds(i, chips, stride=lines), :], norm_rows)
        label_rows = jnp.where(here, wide[pl.ds(half + i, chips, stride=lines), :], label_rows)
    lane = lax.broadcasted_iota(jnp.int32, (rows, TILE), 1)
    chip = lax.broadcasted_iota(jnp.int32, (rows, chips), 1)
    norm_total = jnp.zeros((rows, 1), F32)
    label_total = jnp.zeros((rows, 1), F32)
    for k in range(fanout):
        slot = target[:, k : k + 1]
        at = ones_of(chip == slot // chunk)
        mine = lane == first % TILE + slot % chunk
        for given, which in ((norm_rows, 0), (label_rows, 1)):
            found = jnp.where(mine, contract(at, given.astype(BF16), 1, 0), 0.0)
            found = jnp.sum(found, axis=1, keepdims=True)
            if which == 0:
                norm_total = norm_total + found
            else:
                label_total = label_total + found
    losses = jnp.broadcast_to(jnp.log(norm_total) - label_total, (rows, TILE))
    losses_out[...] = losses.T[0:1, :]


def pull_body(place, stats, notes, raised, share, own, other, out, wide, *, scale, capacity, fanout, per_owner):
    docs, width = own.shape
    rows = notes.shape[1]
    chunk = CORES * capacity
    chips, lines, _ = stats.shape
    wide[...] = stats[...].astype(F32).reshape(chips * lines, TILE)
    at = 2 * per_owner
    chip = lax.broadcasted_iota(jnp.int32, (chips, fanout * TILE), 0).astype(F32)
    line = lax.broadcasted_iota(jnp.int32, (TILE, fanout * TILE), 0)
    lane = lax.broadcasted_iota(jnp.int32, (1, TILE), 1)
    norms = []
    for i in range(rows // TILE):
        span = slice(i * TILE, (i + 1) * TILE)
        source = jnp.concatenate([notes[at + k : at + k + 1, span] for k in range(fanout)], axis=1)
        start = ((i * TILE + lane) // chunk) * chunk
        slot = jnp.concatenate(
            [
                (start + notes[at + fanout + k : at + fanout + k + 1, span].astype(jnp.int32)) % TILE
                for k in range(fanout)
            ],
            axis=1,
        )
        given = wide[pl.ds(i, chips, stride=lines), :].astype(BF16)
        found = jnp.where(line == slot, contract(given, ones_of(chip == source), 0, 0), 0.0)
        found = jnp.sum(found, axis=0, keepdims=True)
        norms.append(sum(found[:, k * TILE : (k + 1) * TILE] for k in range(fanout)))
    norm_total = jnp.concatenate(norms, axis=1)
    high = at + 2 * fanout
    spread = LOSS_SCALE * (raised[...] / norm_total - share[...])
    spread = jnp.where(notes[high : high + 1, :] > 0.0, spread, 0.0)
    core = (lax.broadcasted_iota(jnp.int32, (docs, rows), 1) // capacity) % CORES
    mine = core == place[0]
    near = jnp.where(mine, spread, 0.0).astype(BF16)
    far = jnp.where(mine, 0.0, spread).astype(BF16)
    out[...] = (
        (contract(near, own[...], 0, 0) + contract(far, other[...], 0, 0)) * scale
    ).astype(BF16)


def ready_body(arrived, book, adapter, unit_out, radius_out, raised_out, share_out, *, per_owner):
    exact, radius_out[...] = adapt(arrived[:, : adapter.shape[0]], adapter[...])
    unit_out[...] = exact.astype(BF16)
    index = lax.broadcasted_iota(jnp.int32, raised_out.shape, 0).astype(F32)
    raised_spread = jnp.zeros(raised_out.shape, F32)
    share_spread = jnp.zeros(raised_out.shape, F32)
    first = book.shape[0] - 2 * per_owner
    second = first + per_owner
    for m in range(per_owner):
        here = index == book[m : m + 1, :]
        raised_spread = jnp.where(here, book[first + m : first + m + 1, :], raised_spread)
        share_spread = jnp.where(here, book[second + m : second + m + 1, :], share_spread)
    raised_out[...] = raised_spread
    share_out[...] = share_spread


def terms_body(place, arrived, unit, radius, pulled, keep_out, give_out, terms):
    width = pulled.shape[1]
    pull = pulled[...].astype(F32)
    unit_rows = unit[...].astype(F32)
    projection = jnp.mean(unit_rows * pull, axis=-1, keepdims=True)
    owed = ((pull - unit_rows * projection) / radius[...]).astype(BF16)
    terms[...] = contract(arrived[:, :width], owed, 0, 0)
    lines, _, zs, block, part = keep_out.shape
    core, y, x = place[0], place[1], place[4]
    straight = core == 0
    for whose, out, straight in ((core, keep_out, core == 0), (1 - core, give_out, core != 0)):
        for i in range(lines):
            for l in range(lines):
                row = (y + jnp.where(straight, i, l)) % lines
                column = pl.multiple_of((x + jnp.where(straight, l, i)) % lines * part, TILE)
                for j in range(zs):
                    group = (j * lines + row) * CORES + whose
                    out[i, l, j] = terms[pl.ds(group * block, block), pl.ds(column, part)].astype(BF16)


def grad_body(pulled, target, exact, radius, adapter, query_out):
    placed = sum(placed_of(target[...], pulled.shape[0]))
    pull_total = contract(placed, pulled[...], 1, 0)
    unit_exact = exact[...]
    projection = jnp.mean(unit_exact * pull_total, axis=-1, keepdims=True)
    adapted_grad = ((pull_total - unit_exact * projection) / radius[...]).astype(BF16)
    query_out[...] = contract(adapted_grad, adapter[...], 1, 1).astype(BF16)


def join_body(*refs):
    pieces, out = refs[:-1], refs[-1]
    total = pieces[0][...].astype(F32)
    for one in pieces[1:]:
        total = total + one[...].astype(F32)
    total = total.astype(BF16)
    for r in range(out.shape[1]):
        out[:, r] = total


def settle_body(parts, adapter_out, *, scale):
    zs, reps = parts.shape[:2]
    size = parts.shape[3]
    for r in range(reps):
        columns = parts[0, r].astype(F32)
        for z in range(1, zs):
            columns = columns + parts[z, r].astype(F32)
        adapter_out[:, r * size : (r + 1) * size] = (columns * scale).astype(BF16)


def call(body, name, outs, scratch=(), place=False, limit=None):
    def run(*args):
        specs = [pl.BlockSpec(memory_space=pltpu.VMEM) for _ in args]
        if place:
            specs[0] = pl.BlockSpec(memory_space=pltpu.SMEM)
        return pl.pallas_call(
            body,
            name=name,
            in_specs=specs,
            out_shape=[jax.ShapeDtypeStruct(shape, dtype) for shape, dtype in outs],
            scratch_shapes=list(scratch),
            compiler_params=pltpu.CompilerParams(vmem_limit_bytes=limit),
        )(*args)

    return run


def exchange(rows, chips):
    grouped = rows.reshape(chips, rows.shape[0] // chips, rows.shape[1])
    return lax.all_to_all(grouped, CHIPS, split_axis=0, concat_axis=0, tiled=True).reshape(rows.shape)


def ahead(value, axis, step):
    size = lax.axis_size(axis)
    return lax.ppermute(value, axis, [(i, (i + step) % size) for i in range(size)])


def turned(value, step, first):
    names = ("y", "core", "rep")
    lines = lax.axis_size("y")
    pairs = []
    for y in range(lines):
        for core in range(CORES):
            for x in range(lines):
                along_y = core == first
                to_y = (y + step) % lines if along_y else y
                to_x = x if along_y else (x + step) % lines
                pairs.append(
                    ((y * CORES + core) * lines + x, (to_y * CORES + core) * lines + to_x)
                )
    return lax.ppermute(value, names, pairs)


def added(pieces):
    total = pieces[0].astype(F32)
    for one in pieces[1:]:
        total = total + one.astype(F32)
    return total.astype(BF16)


def on_device(queries, adapter, doc_table, routes, doc_rows, labels):
    cores, reps = lax.axis_size("core"), lax.axis_size("rep")
    ys, zs = lax.axis_size("y"), lax.axis_size("z")
    owners = cores * reps * ys * zs
    chips = owners // cores
    query_rows, width = queries.shape
    fanout = routes.shape[1]
    per_owner = doc_rows.shape[2]
    docs = doc_table.shape[0]
    capacity = max(2, 2 * query_rows * fanout // owners)
    slots = owners * capacity
    scale = 2.0 / math.sqrt(width)
    flat_rows = doc_rows.transpose(1, 2, 0).reshape(fanout * per_owner, query_rows)
    flat_labels = labels.transpose(1, 2, 0).reshape(fanout * per_owner, query_rows)
    at = {name: lax.axis_index(name) for name in EVERY}
    chip = (at["z"] * ys + at["y"]) * reps + at["rep"]
    place = jnp.stack([at["core"], at["y"], at["z"], chip, at["rep"]]).astype(jnp.int32)

    (own,) = call(unit_body, "unit", [((docs, width), BF16)])(doc_table)
    other = ahead(own, "core", 1)
    outgoing, target = call(
        lambda *refs: send_body(*refs, owners=owners, reps=reps, capacity=capacity),
        "send",
        [((slots, width + TILE), BF16), ((query_rows, fanout), jnp.int32)],
    )(queries, routes.T, flat_rows, flat_labels)
    queries, other = lax.optimization_barrier((queries, other))
    exact, radius = call(local_body, "local", [((query_rows, width), F32), ((query_rows, 1), F32)])(
        queries, adapter
    )
    arrived = exchange(outgoing, chips)
    arrived, exact, radius = lax.optimization_barrier((arrived, exact, radius))
    lines = 2 * slots // TILE
    noted = -(-(2 * per_owner + 2 * fanout + 2) // 8) * 8
    stats_out, book = call(
        lambda *refs: score_body(
            *refs, scale=scale, capacity=capacity, fanout=fanout, per_owner=per_owner
        ),
        "score",
        [
            ((chips, lines, TILE), BF16),
            ((noted + 2 * per_owner, slots), F32),
        ],
        place=True,
        limit=32 * 2**20,
    )(place, arrived, adapter, own, other)
    stats = lax.all_to_all(stats_out, CHIPS, split_axis=0, concat_axis=0, tiled=True)
    ready = call(
        lambda *refs: ready_body(*refs, per_owner=per_owner),
        "ready",
        [((slots, width), BF16), ((slots, 1), F32), ((docs, slots), F32), ((docs, slots), F32)],
    )(arrived, book, adapter)
    stats, ready = lax.optimization_barrier((stats, ready))
    held_unit, held_radius, raised, share = ready
    wide = [pltpu.VMEM((chips * lines, TILE), F32)]
    (losses,) = call(
        lambda *refs: loss_body(*refs, chunk=CORES * capacity),
        "loss",
        [((1, query_rows), F32)],
        scratch=wide,
        place=True,
    )(place, stats, target)
    (pull_out,) = call(
        lambda *refs: pull_body(
            *refs, scale=scale, capacity=capacity, fanout=fanout, per_owner=per_owner
        ),
        "pull",
        [((slots, width), BF16)],
        scratch=wide,
        place=True,
    )(place, stats, book, raised, share, own, other)
    pulled = exchange(pull_out, chips)
    block = width // (cores * ys * zs)
    keep, give = call(
        terms_body,
        "terms",
        [((ys, reps, zs, block, width // reps), BF16)] * 2,
        scratch=[pltpu.VMEM((width, width), F32)],
        place=True,
    )(place, arrived, held_unit, held_radius, pull_out)
    taken = ahead(give, "core", 1)
    pair = [(keep[i].astype(F32) + taken[i].astype(F32)).astype(BF16) for i in range(ys)]
    line = [turned(pair[j], j, 0) for j in range(1, ys)]
    line, losses = lax.optimization_barrier((line, losses))
    line = added(pair[:1] + line)
    plane = [line[0]] + [turned(line[j], j, 1) for j in range(1, ys)]
    piece = line.shape[2:]
    (sent,) = call(join_body, "join", [((zs, reps) + piece, BF16)])(*plane)
    sent = sent.reshape((zs * reps,) + piece)
    sent, pulled = lax.optimization_barrier((sent, pulled))
    settled = lax.all_to_all(sent, ("z", "rep"), split_axis=0, concat_axis=0, tiled=True)
    (query_grads,) = call(grad_body, "grad", [((query_rows, width), BF16)])(
        pulled, target, exact, radius, adapter
    )
    (adapter_grad,) = call(
        lambda *refs: settle_body(*refs, scale=1.0 / math.sqrt(query_rows * owners)),
        "settle",
        [((block, width), BF16)],
        limit=16 * 2**20,
    )(settled.reshape((zs, reps) + piece))
    return losses.reshape(query_rows), query_grads, adapter_grad


def solution(mesh):
    groups, reps = mesh.devices.shape
    ys = min(4, groups // CORES)
    fine = Mesh(mesh.devices.reshape(groups // (ys * CORES), ys, CORES, reps), EVERY)
    placed = (
        P(EVERY, None),
        P(),
        P(EVERY, None),
        P(EVERY, None),
        P(EVERY, None, None),
        P(EVERY, None, None),
    )
    return jax.shard_map(
        on_device,
        mesh=fine,
        in_specs=placed,
        out_specs=(P(EVERY), P(EVERY, None), P(DOCS, None)),
        check_vma=False,
    )
```
